32 devices in a mesh: pipe: 8 (over y, x, core), sp: 4 (over z).
Axes of the slice: x: 2, y: 2, z: 4, core: 2. Of those that a mesh axis runs over, the one named last changes fastest.
Arguments:
- queries: bfloat16 [8, 512, 8192], P('pipe', 'sp'), may hold values from -48 to 48, as said below
- keys_values: bfloat16 [8, 512, 2048], P('pipe', 'sp'), may hold values from -8 to 8
- first_tile: int32 [8, 4], P('pipe'), may hold values from 0 to 3, as said below
Outputs:
- next_input: bfloat16 [8, 512, 8192], P('pipe', 'sp')
The draws below stay inside these ranges and needn't reach their ends.
Inputs may be any that keep to these rules, and one draw needn't show every extreme that they name: queries[s, i, :] and keys_values[s, j, :] are of order one in most rows; a few rows are much larger. first_tile[s, t] is the first tile of the document that holds tile t of section s: first_tile[s, 0] = 0, first_tile[s, t] is t or first_tile[s, t - 1], and the last tile 4 - 1 begins a document.
All inputs are finite; a program needn't handle non-finite values.
Results may differ from the reference program's by a relative error of at most 0.0046.
Values may be sent and summed in bfloat16 or wider, within the bound.
A program may use at most 64 MiB of HBM per device.

```python
import math
import jax
import jax.numpy as jnp
from jax import lax

H = 64
KVH = 8
DH = 128
TILE = 128
SEQ = 512
TILES = 4
SECTIONS = 8


def paired_draw(key):
    subkeys = jax.random.split(jax.random.fold_in(key, 17), 2)
    kv_normal = jnp.clip(jax.random.normal(subkeys[0], (SECTIONS, SEQ, KVH, 2, DH), jnp.float32), -4.0, 4.0)
    query_normal = jnp.clip(jax.random.normal(subkeys[1], (SECTIONS, SEQ, H, DH), jnp.float32), -4.0, 4.0)
    keys_only = kv_normal[:, :, :, 0, :]
    values_only = kv_normal[:, :, :, 1, :]
    kv_full = jnp.stack([keys_only, values_only], axis=3).reshape(SECTIONS, SEQ, KVH * 2 * DH)
    return (query_normal.reshape(SECTIONS, SEQ, H * DH), kv_full)


def draw_queries(key, part):
    return paired_draw(key)[0].astype(jnp.bfloat16)


def draw_keys_values(key, part):
    return paired_draw(key)[1].astype(jnp.bfloat16)


def draw_first_tile(key, part):
    flags = jax.random.randint(jax.random.fold_in(key, 29), (SECTIONS, TILES), 0, 4) == 0
    tile_ids = jnp.arange(TILES, dtype=jnp.int32)[None, :]
    flags = flags | (tile_ids == 0) | (tile_ids == TILES - 1)
    starts = jnp.where(flags, tile_ids, 0).astype(jnp.int32)
    return lax.cummax(starts, axis=1).astype(jnp.int32)


def setup_inputs(seed: int = 0) -> dict:
    seeds = jax.random.split(jax.random.key(seed), 4)
    queries = draw_queries(jax.random.fold_in(seeds[3], 71), 0)
    keys_values = draw_keys_values(jax.random.fold_in(seeds[3], 71), 0)
    first_tile = draw_first_tile(jax.random.fold_in(seeds[3], 71), 0)
    return dict(queries=queries, keys_values=keys_values, first_tile=first_tile)


def attend_heads(query_part, key_value_part, row_start):
    seq_len = query_part.shape[0]
    dim_head = query_part.shape[-1]
    block_rows = seq_len // 8
    scale_factor = 1.0 / math.sqrt(dim_head)
    key_part = key_value_part[..., :dim_head].astype(jnp.float32)
    value_part = key_value_part[..., dim_head:].astype(jnp.float32)
    pieces = []
    for block_index in range(8):
        begin_row = block_index * block_rows
        end_row = begin_row + block_rows
        scores = jnp.einsum('ikgd,jkd->kgij', query_part[begin_row:end_row].astype(jnp.float32), key_part[:end_row]) * scale_factor
        row_ids = jnp.arange(begin_row, end_row, dtype=jnp.int32)[:, None]
        col_ids = jnp.arange(end_row, dtype=jnp.int32)[None, :]
        visible = (col_ids <= row_ids) & (col_ids >= row_start[begin_row:end_row][:, None])
        scores = jnp.where(visible, scores, -jnp.inf)
        largest = lax.optimization_barrier(jnp.max(scores, axis=-1, keepdims=True))
        exponent_terms = jnp.exp(scores - largest)
        weights = lax.optimization_barrier((exponent_terms / lax.optimization_barrier(jnp.sum(exponent_terms, axis=-1, keepdims=True))).astype(jnp.bfloat16))
        attended = jnp.einsum('kgij,jkd->ikgd', weights.astype(jnp.float32), value_part[:end_row])
        pieces.append(attended.astype(jnp.bfloat16))
    return jnp.concatenate(pieces, axis=0)

def reference(queries, keys_values, first_tile):
    group_size = H // KVH

    def one_section(section_args):
        section_queries, section_kv, section_first = section_args
        seq_len = section_queries.shape[0]
        row_start = jnp.repeat(section_first * TILE, TILE).astype(jnp.int32)
        query_part = section_queries.reshape(seq_len, KVH, group_size, DH)
        kv_part = section_kv.reshape(seq_len, KVH, 2 * DH)
        return attend_heads(query_part, kv_part, row_start).reshape(seq_len, H * DH)
    attended = lax.map(one_section, (queries, keys_values, first_tile))
    return jnp.roll(attended, 1, axis=0)
```

```python
import functools
import math

import jax
import jax.numpy as jnp
from jax import lax
from jax.experimental import pallas as pl
from jax.experimental.pallas import tpu as pltpu
from jax.sharding import PartitionSpec as P

H = 64
KVH = 8
DH = 128
REP = H // KVH
QW = REP * DH
KW = 2 * DH
UNROLL_TILES = 3
DIRECT = 1
AHEAD = 3
AHEAD_EVEN = 2
TURN_FIRST = 2
TURN_LATER = 3
GIVEN = 1
TAKEN = KVH
SLOTS = KVH + 1
TAKEN_AFTER = 2
MESH = pl.DeviceIdType.MESH


def scores_of(query, key):
    return lax.dot_general(
        query, key, (((1,), (1,)), ((), ())), preferred_element_type=jnp.float32
    )


def attend(queries, keys, values, biases, visible, factor):
    query = jnp.concatenate(queries, axis=0)
    heads = len(queries)
    scores = [scores_of(key, query) for key in keys]
    parts = [score + bias for score, bias in zip(scores, biases)]
    parts.append(jnp.where(jnp.concatenate([visible] * heads, axis=1), scores[-1], -jnp.inf))
    largest = jnp.max(functools.reduce(jnp.maximum, parts), axis=0, keepdims=True)
    terms = [jnp.exp2((part - largest) * factor) for part in parts]
    total = jnp.sum(functools.reduce(jnp.add, terms), axis=0, keepdims=True)
    result = sum(
        jnp.dot(value.T, term.astype(jnp.bfloat16), preferred_element_type=jnp.float32)
        for value, term in zip(values, terms)
    ) * (1.0 / total)
    rows = queries[0].shape[0]
    return [
        result[:, head * rows:(head + 1) * rows].T.astype(jnp.bfloat16) for head in range(heads)
    ]


def kernel(n_pipe, n_sp, first_hbm, q_hbm, kv_hbm, out_ref, first_ref, first_taken, first_now, q_buf, own,
           kv_buf, staged, turn, first_sem, q_sem, own_sem, direct_send, kv_send, kv_recv,
           give_send, give_recv, taken_sem, out_send, out_recv):
    sp = lax.axis_index("sp")
    pipe = lax.axis_index("pipe")
    after = lax.rem(pipe + 1, n_pipe)
    before = lax.rem(pipe + n_pipe - 1, n_pipe)
    rows = q_hbm.shape[1]
    last = n_sp - 1
    n_before = jnp.where(sp == last, 0, sp)
    sends = sp < last - 1
    paired = n_pipe % 2 == 0
    odd = lax.rem(pipe, 2) == 1
    even = jnp.logical_not(odd)
    gives = odd & (n_before > 0) & paired
    takes = even & (n_before > 0) & paired
    ahead = jnp.where(odd, AHEAD, AHEAD_EVEN)
    turn_group = jnp.where(sp == 0, TURN_FIRST, TURN_LATER)

    def q_cols(g, count=1):
        return pl.ds(pl.multiple_of(g * QW, QW), count * QW)

    def kv_cols(g, count=1):
        return pl.ds(pl.multiple_of(g * KW, KW), count * KW)

    def loads(g, count):
        q, kv = q_cols(g, count), kv_cols(g, count)
        index = 0 if g == 0 else 1
        return [
            pltpu.make_async_copy(kv_hbm.at[0, :, kv], own.at[:, kv], own_sem.at[index]),
            pltpu.make_async_copy(q_hbm.at[0, :, q], q_buf.at[:, q], q_sem.at[index]),
        ]

    def kv_copy(g, source, tile, target, send_sem, count=1):
        cols = kv_cols(g, count)
        return pltpu.make_async_remote_copy(
            src_ref=source.at[:, cols],
            dst_ref=kv_buf.at[tile, :, cols],
            send_sem=send_sem,
            recv_sem=kv_recv.at[tile, g],
            device_id={"sp": target},
            device_id_type=MESH,
        )

    def own_send(g, count=1):
        return kv_copy(g, kv_hbm.at[0], sp, sp + 1, kv_send.at[0], count)

    def direct(g, target):
        return kv_copy(g, kv_hbm.at[0], sp, target, direct_send.at[target - 2])

    def forward(g, tile, count=1):
        return kv_copy(g, kv_buf.at[tile], tile, sp + 1, kv_send.at[tile + 1], count)

    def arrival(g, tile):
        return kv_copy(g, kv_buf.at[tile], tile, sp, kv_send.at[tile + 1])

    def give(source, target, index):
        return pltpu.make_async_remote_copy(
            src_ref=source, dst_ref=target, send_sem=give_send.at[index],
            recv_sem=give_recv.at[index], device_id={"pipe": after}, device_id_type=MESH,
        )

    def gifts():
        return [
            give(q_hbm.at[0, :, q_cols(GIVEN)], q_buf.at[:, q_cols(TAKEN)], 0),
            give(kv_hbm.at[0, :, kv_cols(GIVEN)], own.at[:, kv_cols(TAKEN)], 1),
            give(first_hbm, first_taken, 2),
        ]

    def give_tile(tile):
        return give(
            kv_buf.at[tile, :, kv_cols(GIVEN)], kv_buf.at[tile, :, kv_cols(TAKEN)], 3 + tile
        )

    def out_copy(g, count=1):
        cols = q_cols(g, count)
        return pltpu.make_async_remote_copy(
            src_ref=staged.at[:, cols],
            dst_ref=out_ref.at[0, :, cols],
            send_sem=out_send,
            recv_sem=out_recv,
            device_id={"pipe": after},
            device_id_type=MESH,
        )

    taken_copy = pltpu.make_async_copy(
        staged.at[:, q_cols(TAKEN)], out_ref.at[0, :, q_cols(GIVEN)], taken_sem
    )
    barrier = pltpu.get_barrier_semaphore()
    for neighbour in (after, before):
        pl.semaphore_signal(barrier, inc=1, device_id={"pipe": neighbour}, device_id_type=MESH)
    for step in range(1, last):
        @pl.when(sp < last)
        def _():
            pl.semaphore_signal(
                barrier, inc=1, device_id={"sp": lax.rem(sp + step, last)}, device_id_type=MESH
            )
    for load in loads(0, 1):
        load.start()
    first_copy = pltpu.make_async_copy(first_hbm, first_ref, first_sem)
    first_copy.start()

    def send_own(g):
        @pl.when(sends)
        def _():
            if isinstance(g, int) and g < DIRECT:
                for target in range(last - 1, 1, -1):
                    @pl.when(target > sp + 1)
                    def _():
                        direct(g, target).start()
            own_send(g).start()

    def enter():
        pl.semaphore_wait(barrier, jnp.where(sp < last, last + 1, 2))
        if paired:
            @pl.when(gives)
            def _():
                for gift in gifts():
                    gift.start()

            @pl.when(sends & even)
            def _():
                pl.semaphore_wait(turn, 1)
        for g in range(DIRECT):
            send_own(g)

        @pl.loop(DIRECT, jnp.where(sp == 0, KVH, ahead))
        def _(g):
            send_own(g)

    def rest_of_loads():
        for load in loads(1, KVH - 1):
            load.start()

    @pl.when(n_before > 0)
    def _():
        enter()
        rest_of_loads()
        first_copy.wait()

    factor = math.log2(math.e) / math.sqrt(DH)
    row_ids = lax.broadcasted_iota(jnp.int32, (rows, rows), 0)
    col_ids = lax.broadcasted_iota(jnp.int32, (rows, rows), 1)

    first_now[0] = 0

    def choose_first(g):
        @pl.when((n_before > 0) & (g < KVH))
        def _():
            first_now[0] = first_ref[0, sp]

        @pl.when(g == TAKEN)
        def _():
            first_now[0] = first_taken[0, sp]

    def bias_of(tile, first):
        return jnp.where(tile >= first, 0.0, -jnp.inf).astype(jnp.float32)

    def whole_softmax(g, count):
        k_cols = pl.ds(pl.multiple_of(g * KW, DH), DH)
        v_cols = pl.ds(pl.multiple_of(g * KW + DH, DH), DH)
        cols = [
            pl.ds(pl.multiple_of(g * QW + head * DH, DH), DH)
            for head in range(REP)
        ]
        first = first_now[0] if count else None
        results = attend(
            [q_buf[:, c] for c in cols],
            [kv_buf[tile, :, k_cols] for tile in range(count)] + [own[:, k_cols]],
            [kv_buf[tile, :, v_cols] for tile in range(count)] + [own[:, v_cols]],
            [bias_of(tile, first) for tile in range(count)],
            row_ids <= col_ids, factor,
        )
        for c, result in zip(cols, results):
            staged[:, c] = result

    def running_softmax(g):
        k_cols = pl.ds(pl.multiple_of(g * KW, DH), DH)
        v_cols = pl.ds(pl.multiple_of(g * KW + DH, DH), DH)
        first = first_now[0]

        @pl.loop(0, REP)
        def _(head):
            cols = pl.ds(pl.multiple_of(g * QW + head * DH, DH), DH)
            query = q_buf[:, cols]
            score = jnp.where(col_ids <= row_ids, scores_of(query, own[:, k_cols]), -jnp.inf)
            largest = jnp.max(score, axis=-1, keepdims=True)
            term = jnp.exp2((score - largest) * factor)
            total = jnp.sum(term, axis=-1, keepdims=True)
            result = jnp.dot(term.astype(jnp.bfloat16), own[:, v_cols],
                             preferred_element_type=jnp.float32)

            def step(tile, carry):
                largest, total, result = carry
                score = scores_of(query, kv_buf[tile, :, k_cols]) + bias_of(tile, first)
                larger = jnp.maximum(largest, jnp.max(score, axis=-1, keepdims=True))
                shrink = jnp.exp2((largest - larger) * factor)
                term = jnp.exp2((score - larger) * factor)
                total = total * shrink + jnp.sum(term, axis=-1, keepdims=True)
                result = result * shrink + jnp.dot(
                    term.astype(jnp.bfloat16), kv_buf[tile, :, v_cols],
                    preferred_element_type=jnp.float32)
                return larger, total, result

            _, total, result = lax.fori_loop(0, n_before, step, (largest, total, result))
            staged[:, cols] = (result / total).astype(jnp.bfloat16)

    def arrive(g):
        for tile in range(last - 1):
            @pl.when(tile < n_before)
            def _():
                arrival(g, tile).wait_recv()

                @pl.when(sends & (g >= DIRECT))
                def _():
                    forward(g, tile).start()

                @pl.when(gives & (g == GIVEN))
                def _():
                    give_tile(tile).start()

        @pl.when((sp > 0) & (g + ahead < KVH))
        def _():
            send_own(g + ahead)
        for wanted, count in ((0, 1), (1, KVH - 1)):
            @pl.when(g == wanted)
            def _():
                for load in loads(wanted, count):
                    load.wait()

    def taken_arrive():
        for gift in gifts():
            gift.wait_recv()
        for tile in range(last - 1):
            @pl.when(tile < n_before)
            def _():
                give_tile(tile).wait_recv()

    def finished(i, g, entering):
        if entering:
            @pl.when((i == 1) & (n_before == 0))
            def _():
                enter()

        @pl.when(g < KVH)
        def _():
            out_copy(g).start()

        @pl.when(g == TAKEN)
        def _():
            taken_copy.start()
        if entering:
            @pl.when((i == 1) & (n_before == 0))
            def _():
                rest_of_loads()

    def group(i):
        shift = jnp.where(takes & (i > TAKEN_AFTER), 2, 1)
        g = jnp.where(takes & (i == TAKEN_AFTER + 1), TAKEN, i - shift)

        @pl.when(g < KVH)
        def _():
            arrive(g)

        if paired:
            @pl.when(g == TAKEN)
            def _():
                taken_arrive()

        choose_first(g)
        computes = jnp.logical_not(gives & (g == GIVEN))
        if last <= UNROLL_TILES:
            for count in range(max(last, 1)):
                @pl.when((n_before == count) & computes)
                def _():
                    whole_softmax(g, count)
                    finished(i, g, count == 0)
        else:
            @pl.when(computes)
            def _():
                running_softmax(g)
                finished(i, g, True)
        if paired:
            @pl.when(sends & odd & (g == turn_group))
            def _():
                pl.semaphore_signal(
                    turn, inc=1, device_id={"pipe": before}, device_id_type=MESH
                )

    @pl.loop(1, jnp.where(takes, KVH + 2, KVH + 1))
    def _(i):
        group(i)

    @pl.when(n_before == 0)
    def _():
        first_copy.wait()
    for g in range(DIRECT):
        for target in range(last - 1, 1, -1):
            @pl.when(target > sp + 1)
            def _():
                direct(g, target).wait_send()
    if paired:
        @pl.when(gives)
        def _():
            for gift in gifts():
                gift.wait_send()
            for tile in range(last - 1):
                @pl.when(tile < n_before)
                def _():
                    give_tile(tile).wait_send()

        @pl.when(takes)
        def _():
            taken_copy.wait()

    @pl.when(sends)
    def _():
        own_send(0, KVH).wait_send()
    for tile in range(last - 1):
        @pl.when(sends & (tile < n_before))
        def _():
            forward(DIRECT, tile, KVH - DIRECT).wait_send()

    @pl.when(gives)
    def _():
        out_copy(0, KVH - 1).wait_send()

    @pl.when(jnp.logical_not(gives))
    def _():
        out_copy(0, KVH).wait_send()

    @pl.when(takes)
    def _():
        out_copy(0, KVH - 1).wait_recv()

    @pl.when(jnp.logical_not(takes))
    def _():
        out_copy(0, KVH).wait_recv()


def per_device(n_pipe, n_sp, queries, keys_values, first_tile):
    rows = queries.shape[1]
    tiles = n_sp
    return pl.pallas_call(
        functools.partial(kernel, n_pipe, n_sp),
        out_shape=jax.ShapeDtypeStruct(queries.shape, jnp.bfloat16),
        in_specs=[
            pl.BlockSpec(memory_space=pltpu.HBM),
            pl.BlockSpec(memory_space=pltpu.HBM),
            pl.BlockSpec(memory_space=pltpu.HBM),
        ],
        out_specs=pl.BlockSpec(memory_space=pl.ANY),
        scratch_shapes=[
            pltpu.SMEM(first_tile.shape, jnp.int32),
            pltpu.SMEM(first_tile.shape, jnp.int32),
            pltpu.SMEM((1,), jnp.int32),
            pltpu.VMEM((rows, SLOTS * QW), jnp.bfloat16),
            pltpu.VMEM((rows, SLOTS * KW), jnp.bfloat16),
            pltpu.VMEM((max(tiles - 2, 1), rows, SLOTS * KW), jnp.bfloat16),
            pltpu.VMEM((rows, SLOTS * QW), jnp.bfloat16),
            pltpu.SemaphoreType.REGULAR,
            pltpu.SemaphoreType.DMA,
            pltpu.SemaphoreType.DMA((2,)),
            pltpu.SemaphoreType.DMA((2,)),
            pltpu.SemaphoreType.DMA((max(tiles - 3, 1),)),
            pltpu.SemaphoreType.DMA((tiles - 1,)),
            pltpu.SemaphoreType.DMA((max(tiles - 2, 1), KVH)),
            pltpu.SemaphoreType.DMA((3 + max(tiles - 2, 1),)),
            pltpu.SemaphoreType.DMA((3 + max(tiles - 2, 1),)),
            pltpu.SemaphoreType.DMA,
            pltpu.SemaphoreType.DMA,
            pltpu.SemaphoreType.DMA,
        ],
        compiler_params=pltpu.CompilerParams(
            collective_id=0, has_side_effects=True, vmem_limit_bytes=40 * 1024 * 1024
        ),
    )(
        pltpu.with_memory_space_constraint(first_tile, pltpu.HBM),
        pltpu.with_memory_space_constraint(queries, pltpu.HBM),
        pltpu.with_memory_space_constraint(keys_values, pltpu.HBM),
    )


def solution(mesh):
    sizes = dict(mesh.shape)
    in_specs = (P("pipe", "sp", None), P("pipe", "sp", None), P("pipe", None))
    out_specs = P("pipe", "sp", None)
    return jax.shard_map(
        functools.partial(per_device, sizes["pipe"], sizes["sp"]),
        mesh=mesh, in_specs=in_specs, out_specs=out_specs, check_vma=False,
    )
```

```python
import functools
import math

import jax
import jax.numpy as jnp
from jax import lax
from jax.experimental import pallas as pl
from jax.experimental.pallas import tpu as pltpu
from jax.sharding import PartitionSpec as P

H = 64
KVH = 8
DH = 128
REP = H // KVH
QW = REP * DH
KW = 2 * DH
UNROLL_TILES = 3
DIRECT = 1
AHEAD = 4
AHEAD_EVEN = 2
TURN_FIRST = 2
TURN_LATER = 5
GIVEN = 1
TAKEN = KVH
SLOTS = KVH + 1
TAKEN_AFTER = 2
RELAYED = 3
RELAYED_HEADS = 5
RW = RELAYED_HEADS * DH
MESH = pl.DeviceIdType.MESH


def scores_of(query, key):
    return lax.dot_general(
        query, key, (((1,), (1,)), ((), ())), preferred_element_type=jnp.float32
    )


def attend(queries, keys, values, biases, visible, factor):
    query = jnp.concatenate(queries, axis=0)
    heads = len(queries)
    scores = [scores_of(key, query) for key in keys]
    parts = [score + bias for score, bias in zip(scores, biases)]
    parts.append(jnp.where(jnp.concatenate([visible] * heads, axis=1), scores[-1], -jnp.inf))
    largest = jnp.max(functools.reduce(jnp.maximum, parts), axis=0, keepdims=True)
    terms = [jnp.exp2((part - largest) * factor) for part in parts]
    total = jnp.sum(functools.reduce(jnp.add, terms), axis=0, keepdims=True)
    result = sum(
        jnp.dot(value.T, term.astype(jnp.bfloat16), preferred_element_type=jnp.float32)
        for value, term in zip(values, terms)
    ) * (1.0 / total)
    rows = queries[0].shape[0]
    return [
        result[:, head * rows:(head + 1) * rows].T.astype(jnp.bfloat16) for head in range(heads)
    ]


def kernel(n_pipe, n_sp, first_hbm, q_hbm, kv_hbm, out_ref, first_ref, first_taken, first_now, q_buf, own,
           kv_buf, staged, relay_buf, turn, first_sem, q_sem, own_sem, direct_send, kv_send, kv_recv,
           give_send, give_recv, taken_sem, relay_sems, out_send, out_recv):
    sp = lax.axis_index("sp")
    pipe = lax.axis_index("pipe")
    after = lax.rem(pipe + 1, n_pipe)
    before = lax.rem(pipe + n_pipe - 1, n_pipe)
    rows = q_hbm.shape[1]
    last = n_sp - 1
    n_before = jnp.where(sp == last, 0, sp)
    sends = sp < last - 1
    paired = n_pipe % 2 == 0
    odd = lax.rem(pipe, 2) == 1
    even = jnp.logical_not(odd)
    gives = odd & (n_before > 0) & paired
    takes = even & (n_before > 0) & paired
    relaying = paired and last > 1
    relays = odd & (sp == last - 1) & relaying
    carries = even & (sp == last) & relaying
    relayed = even & (sp == last - 1) & relaying
    ahead = jnp.where(odd, AHEAD, AHEAD_EVEN)
    turn_group = jnp.where(sp == 0, TURN_FIRST, TURN_LATER)

    def q_cols(g, count=1):
        return pl.ds(pl.multiple_of(g * QW, QW), count * QW)

    def kv_cols(g, count=1):
        return pl.ds(pl.multiple_of(g * KW, KW), count * KW)

    def loads(g, count):
        q, kv = q_cols(g, count), kv_cols(g, count)
        index = 0 if g == 0 else 1
        return [
            pltpu.make_async_copy(kv_hbm.at[0, :, kv], own.at[:, kv], own_sem.at[index]),
            pltpu.make_async_copy(q_hbm.at[0, :, q], q_buf.at[:, q], q_sem.at[index]),
        ]

    def kv_copy(g, source, tile, target, send_sem, count=1):
        cols = kv_cols(g, count)
        return pltpu.make_async_remote_copy(
            src_ref=source.at[:, cols],
            dst_ref=kv_buf.at[tile, :, cols],
            send_sem=send_sem,
            recv_sem=kv_recv.at[tile, g],
            device_id={"sp": target},
            device_id_type=MESH,
        )

    def own_send(g, count=1):
        return kv_copy(g, kv_hbm.at[0], sp, sp + 1, kv_send.at[0], count)

    def direct(g, target):
        return kv_copy(g, kv_hbm.at[0], sp, target, direct_send.at[target - 2])

    def forward(g, tile, count=1):
        return kv_copy(g, kv_buf.at[tile], tile, sp + 1, kv_send.at[tile + 1], count)

    def arrival(g, tile):
        return kv_copy(g, kv_buf.at[tile], tile, sp, kv_send.at[tile + 1])

    def give(source, target, index):
        return pltpu.make_async_remote_copy(
            src_ref=source, dst_ref=target, send_sem=give_send.at[index],
            recv_sem=give_recv.at[index], device_id={"pipe": after}, device_id_type=MESH,
        )

    def gifts():
        return [
            give(q_hbm.at[0, :, q_cols(GIVEN)], q_buf.at[:, q_cols(TAKEN)], 0),
            give(kv_hbm.at[0, :, kv_cols(GIVEN)], own.at[:, kv_cols(TAKEN)], 1),
            give(first_hbm, first_taken, 2),
        ]

    def give_tile(tile):
        return give(
            kv_buf.at[tile, :, kv_cols(GIVEN)], kv_buf.at[tile, :, kv_cols(TAKEN)], 3 + tile
        )

    def out_copy(begin, width):
        cols = pl.ds(pl.multiple_of(begin, DH), width)
        return pltpu.make_async_remote_copy(
            src_ref=staged.at[:, cols],
            dst_ref=out_ref.at[0, :, cols],
            send_sem=out_send,
            recv_sem=out_recv,
            device_id={"pipe": after},
            device_id_type=MESH,
        )

    relay_cols = pl.ds(RELAYED * QW, RW)
    relay_in = pltpu.make_async_remote_copy(
        src_ref=staged.at[:, relay_cols],
        dst_ref=relay_buf,
        send_sem=relay_sems.at[0],
        recv_sem=relay_sems.at[1],
        device_id={"pipe": after, "sp": last},
        device_id_type=MESH,
    )
    relay_out = pltpu.make_async_remote_copy(
        src_ref=relay_buf,
        dst_ref=out_ref.at[0, :, relay_cols],
        send_sem=relay_sems.at[2],
        recv_sem=relay_sems.at[3],
        device_id={"sp": last - 1},
        device_id_type=MESH,
    )

    def send_out(g):
        split = relays & (g == RELAYED)

        @pl.when(jnp.logical_not(split))
        def _():
            out_copy(g * QW, QW).start()

        if relaying:
            @pl.when(split)
            def _():
                out_copy(RELAYED * QW + RW, QW - RW).start()
                relay_in.start()

    taken_copy = pltpu.make_async_copy(
        staged.at[:, q_cols(TAKEN)], out_ref.at[0, :, q_cols(GIVEN)], taken_sem
    )
    barrier = pltpu.get_barrier_semaphore()

    def greet(**where):
        pl.semaphore_signal(barrier, inc=1, device_id=where, device_id_type=MESH)

    for lower in range(last - 1):
        @pl.when((sp > lower) & (sp < last))
        def _():
            greet(sp=lower)
    greet(pipe=before)
    if paired:
        @pl.when(even)
        def _():
            greet(pipe=after)
    if relaying:
        @pl.when(carries)
        def _():
            greet(pipe=before, sp=last - 1)

        @pl.when(relayed)
        def _():
            greet(sp=last)
    greeted = 1 + jnp.where(sp < last, last - 1 - sp, 0)
    if paired:
        greeted += jnp.where(odd, 1, 0)
    if relaying:
        greeted += jnp.where(relays | carries, 1, 0)
    for load in loads(0, 1):
        load.start()
    first_copy = pltpu.make_async_copy(first_hbm, first_ref, first_sem)
    first_copy.start()

    def send_own(g):
        @pl.when(sends)
        def _():
            if isinstance(g, int) and g < DIRECT:
                for target in range(last - 1, 1, -1):
                    @pl.when(target > sp + 1)
                    def _():
                        direct(g, target).start()
            own_send(g).start()

    def enter():
        pl.semaphore_wait(barrier, greeted)
        if paired:
            @pl.when(gives)
            def _():
                for gift in gifts():
                    gift.start()

            @pl.when(sends & even)
            def _():
                pl.semaphore_wait(turn, 1)
        for g in range(DIRECT):
            send_own(g)

        @pl.loop(DIRECT, jnp.where(sp == 0, KVH, ahead))
        def _(g):
            send_own(g)

    def rest_of_loads():
        for load in loads(1, KVH - 1):
            load.start()

    @pl.when(n_before > 0)
    def _():
        enter()
        rest_of_loads()
        first_copy.wait()

    factor = math.log2(math.e) / math.sqrt(DH)
    row_ids = lax.broadcasted_iota(jnp.int32, (rows, rows), 0)
    col_ids = lax.broadcasted_iota(jnp.int32, (rows, rows), 1)

    first_now[0] = 0

    def choose_first(g):
        @pl.when((n_before > 0) & (g < KVH))
        def _():
            first_now[0] = first_ref[0, sp]

        @pl.when(g == TAKEN)
        def _():
            first_now[0] = first_taken[0, sp]

    def bias_of(tile, first):
        return jnp.where(tile >= first, 0.0, -jnp.inf).astype(jnp.float32)

    def whole_softmax(g, count):
        k_cols = pl.ds(pl.multiple_of(g * KW, DH), DH)
        v_cols = pl.ds(pl.multiple_of(g * KW + DH, DH), DH)
        cols = [
            pl.ds(pl.multiple_of(g * QW + head * DH, DH), DH)
            for head in range(REP)
        ]
        first = first_now[0] if count else None
        results = attend(
            [q_buf[:, c] for c in cols],
            [kv_buf[tile, :, k_cols] for tile in range(count)] + [own[:, k_cols]],
            [kv_buf[tile, :, v_cols] for tile in range(count)] + [own[:, v_cols]],
            [bias_of(tile, first) for tile in range(count)],
            row_ids <= col_ids, factor,
        )
        for c, result in zip(cols, results):
            staged[:, c] = result

    def running_softmax(g):
        k_cols = pl.ds(pl.multiple_of(g * KW, DH), DH)
        v_cols = pl.ds(pl.multiple_of(g * KW + DH, DH), DH)
        first = first_now[0]

        @pl.loop(0, REP)
        def _(head):
            cols = pl.ds(pl.multiple_of(g * QW + head * DH, DH), DH)
            query = q_buf[:, cols]
            score = jnp.where(col_ids <= row_ids, scores_of(query, own[:, k_cols]), -jnp.inf)
            largest = jnp.max(score, axis=-1, keepdims=True)
            term = jnp.exp2((score - largest) * factor)
            total = jnp.sum(term, axis=-1, keepdims=True)
            result = jnp.dot(term.astype(jnp.bfloat16), own[:, v_cols],
                             preferred_element_type=jnp.float32)

            def step(tile, carry):
                largest, total, result = carry
                score = scores_of(query, kv_buf[tile, :, k_cols]) + bias_of(tile, first)
                larger = jnp.maximum(largest, jnp.max(score, axis=-1, keepdims=True))
                shrink = jnp.exp2((largest - larger) * factor)
                term = jnp.exp2((score - larger) * factor)
                total = total * shrink + jnp.sum(term, axis=-1, keepdims=True)
                result = result * shrink + jnp.dot(
                    term.astype(jnp.bfloat16), kv_buf[tile, :, v_cols],
                    preferred_element_type=jnp.float32)
                return larger, total, result

            _, total, result = lax.fori_loop(0, n_before, step, (largest, total, result))
            staged[:, cols] = (result / total).astype(jnp.bfloat16)

    def arrive(g):
        for tile in range(last - 1):
            @pl.when(tile < n_before)
            def _():
                arrival(g, tile).wait_recv()

                @pl.when(sends & (g >= DIRECT))
                def _():
                    forward(g, tile).start()

                @pl.when(gives & (g == GIVEN))
                def _():
                    give_tile(tile).start()

        @pl.when((sp > 0) & (g + ahead < KVH))
        def _():
            send_own(g + ahead)
        for wanted, count in ((0, 1), (1, KVH - 1)):
            @pl.when(g == wanted)
            def _():
                for load in loads(wanted, count):
                    load.wait()

    def taken_arrive():
        for gift in gifts():
            gift.wait_recv()
        for tile in range(last - 1):
            @pl.when(tile < n_before)
            def _():
                give_tile(tile).wait_recv()

    def finished(i, g, entering):
        if entering:
            @pl.when((i == 1) & (n_before == 0))
            def _():
                enter()

        @pl.when(g < KVH)
        def _():
            send_out(g)

        @pl.when(g == TAKEN)
        def _():
            taken_copy.start()
        if entering:
            @pl.when((i == 1) & (n_before == 0))
            def _():
                rest_of_loads()

    def group(i):
        shift = jnp.where(takes & (i > TAKEN_AFTER), 2, 1)
        g = jnp.where(takes & (i == TAKEN_AFTER + 1), TAKEN, i - shift)

        @pl.when(g < KVH)
        def _():
            arrive(g)

        if paired:
            @pl.when(g == TAKEN)
            def _():
                taken_arrive()

        choose_first(g)
        computes = jnp.logical_not(gives & (g == GIVEN))
        if last <= UNROLL_TILES:
            for count in range(max(last, 1)):
                @pl.when((n_before == count) & computes)
                def _():
                    whole_softmax(g, count)
                    finished(i, g, count == 0)
        else:
            @pl.when(computes)
            def _():
                running_softmax(g)
                finished(i, g, True)
        if paired:
            @pl.when(sends & odd & (g == turn_group))
            def _():
                pl.semaphore_signal(
                    turn, inc=1, device_id={"pipe": before}, device_id_type=MESH
                )

    @pl.loop(1, jnp.where(takes, KVH + 2, KVH + 1))
    def _(i):
        group(i)

    @pl.when(n_before == 0)
    def _():
        first_copy.wait()
    for g in range(DIRECT):
        for target in range(last - 1, 1, -1):
            @pl.when(target > sp + 1)
            def _():
                direct(g, target).wait_send()
    if paired:
        @pl.when(gives)
        def _():
            for gift in gifts():
                gift.wait_send()
            for tile in range(last - 1):
                @pl.when(tile < n_before)
                def _():
                    give_tile(tile).wait_send()

        @pl.when(takes)
        def _():
            taken_copy.wait()

    @pl.when(sends)
    def _():
        own_send(0, KVH).wait_send()
    for tile in range(last - 1):
        @pl.when(sends & (tile < n_before))
        def _():
            forward(DIRECT, tile, KVH - DIRECT).wait_send()

    if relaying:
        @pl.when(carries)
        def _():
            relay_in.wait_recv()
            relay_out.start()
            relay_out.wait_send()

        @pl.when(relays)
        def _():
            relay_in.wait_send()

        @pl.when(relayed)
        def _():
            relay_out.wait_recv()

    for given, cut, width in (
        (gives, relays, KVH * QW - QW - RW),
        (gives, jnp.logical_not(relays), KVH * QW - QW),
        (jnp.logical_not(gives), True, KVH * QW),
    ):
        @pl.when(given & cut)
        def _():
            out_copy(0, width).wait_send()

    for taken, cut, width in (
        (takes, relayed, KVH * QW - QW - RW),
        (takes, jnp.logical_not(relayed), KVH * QW - QW),
        (jnp.logical_not(takes), True, KVH * QW),
    ):
        @pl.when(taken & cut)
        def _():
            out_copy(0, width).wait_recv()


def per_device(n_pipe, n_sp, queries, keys_values, first_tile):
    rows = queries.shape[1]
    tiles = n_sp
    return pl.pallas_call(
        functools.partial(kernel, n_pipe, n_sp),
        out_shape=jax.ShapeDtypeStruct(queries.shape, jnp.bfloat16),
        in_specs=[
            pl.BlockSpec(memory_space=pltpu.HBM),
            pl.BlockSpec(memory_space=pltpu.HBM),
            pl.BlockSpec(memory_space=pltpu.HBM),
        ],
        out_specs=pl.BlockSpec(memory_space=pl.ANY),
        scratch_shapes=[
            pltpu.SMEM(first_tile.shape, jnp.int32),
            pltpu.SMEM(first_tile.shape, jnp.int32),
            pltpu.SMEM((1,), jnp.int32),
            pltpu.VMEM((rows, SLOTS * QW), jnp.bfloat16),
            pltpu.VMEM((rows, SLOTS * KW), jnp.bfloat16),
            pltpu.VMEM((max(tiles - 2, 1), rows, SLOTS * KW), jnp.bfloat16),
            pltpu.VMEM((rows, SLOTS * QW), jnp.bfloat16),
            pltpu.VMEM((rows, RW), jnp.bfloat16),
            pltpu.SemaphoreType.REGULAR,
            pltpu.SemaphoreType.DMA,
            pltpu.SemaphoreType.DMA((2,)),
            pltpu.SemaphoreType.DMA((2,)),
            pltpu.SemaphoreType.DMA((max(tiles - 3, 1),)),
            pltpu.SemaphoreType.DMA((tiles - 1,)),
            pltpu.SemaphoreType.DMA((max(tiles - 2, 1), KVH)),
            pltpu.SemaphoreType.DMA((3 + max(tiles - 2, 1),)),
            pltpu.SemaphoreType.DMA((3 + max(tiles - 2, 1),)),
            pltpu.SemaphoreType.DMA,
            pltpu.SemaphoreType.DMA((4,)),
            pltpu.SemaphoreType.DMA,
            pltpu.SemaphoreType.DMA,
        ],
        compiler_params=pltpu.CompilerParams(
            collective_id=0, has_side_effects=True, vmem_limit_bytes=40 * 1024 * 1024
        ),
    )(
        pltpu.with_memory_space_constraint(first_tile, pltpu.HBM),
        pltpu.with_memory_space_constraint(queries, pltpu.HBM),
        pltpu.with_memory_space_constraint(keys_values, pltpu.HBM),
    )


def solution(mesh):
    sizes = dict(mesh.shape)
    in_specs = (P("pipe", "sp", None), P("pipe", "sp", None), P("pipe", None))
    out_specs = P("pipe", "sp", None)
    return jax.shard_map(
        functools.partial(per_device, sizes["pipe"], sizes["sp"]),
        mesh=mesh, in_specs=in_specs, out_specs=out_specs, check_vma=False,
    )
```

```python
import functools
import math

import jax
import jax.numpy as jnp
from jax import lax
from jax.experimental import pallas as pl
from jax.experimental.pallas import tpu as pltpu
from jax.sharding import PartitionSpec as P

H = 64
KVH = 8
DH = 128
REP = H // KVH
QW = REP * DH
KW = 2 * DH
UNROLL_TILES = 3
DIRECT = 0
OWN_FIRST = True
FIRST_HEADS = 4
AHEAD = 4
AHEAD_EVEN = 2
TURN_FIRST = 2
TURN_LATER = 5
GIVEN = 1
TAKEN = KVH
SLOTS = KVH + 1
TAKEN_AFTER = 2
RELAYED = 3
RELAYED_HEADS = 6
RW = RELAYED_HEADS * DH
MESH = pl.DeviceIdType.MESH


def scores_of(query, key):
    return lax.dot_general(
        query, key, (((1,), (1,)), ((), ())), preferred_element_type=jnp.float32
    )


def attend(queries, keys, values, biases, visible, factor):
    query = jnp.concatenate(queries, axis=0)
    heads = len(queries)
    scores = [scores_of(key, query) for key in keys]
    parts = [score + bias for score, bias in zip(scores, biases)]
    parts.append(jnp.where(jnp.concatenate([visible] * heads, axis=1), scores[-1], -jnp.inf))
    largest = jnp.max(functools.reduce(jnp.maximum, parts), axis=0, keepdims=True)
    terms = [jnp.exp2((part - largest) * factor) for part in parts]
    total = jnp.sum(functools.reduce(jnp.add, terms), axis=0, keepdims=True)
    result = sum(
        jnp.dot(value.T, term.astype(jnp.bfloat16), preferred_element_type=jnp.float32)
        for value, term in zip(values, terms)
    ) * (1.0 / total)
    rows = queries[0].shape[0]
    return [
        result[:, head * rows:(head + 1) * rows].T.astype(jnp.bfloat16) for head in range(heads)
    ]


def kernel(n_pipe, n_sp, first_hbm, q_hbm, kv_hbm, out_ref, first_ref, first_taken, first_now, q_buf, own,
           kv_buf, staged, relay_buf, turn, first_sem, q_sem, own_sem, direct_send, kv_send, kv_recv,
           give_send, give_recv, taken_sem, relay_sems, out_send, out_recv):
    sp = lax.axis_index("sp")
    pipe = lax.axis_index("pipe")
    after = lax.rem(pipe + 1, n_pipe)
    before = lax.rem(pipe + n_pipe - 1, n_pipe)
    rows = q_hbm.shape[1]
    last = n_sp - 1
    n_before = jnp.where(sp == last, 0, sp)
    sends = sp < last - 1
    paired = n_pipe % 2 == 0
    odd = lax.rem(pipe, 2) == 1
    even = jnp.logical_not(odd)
    gives = odd & (n_before > 0) & paired
    takes = even & (n_before > 0) & paired
    relaying = paired and last > 1
    relays = odd & (sp == last - 1) & relaying
    carries = even & (sp == last) & relaying
    relayed = even & (sp == last - 1) & relaying
    ahead = jnp.where(odd, AHEAD, AHEAD_EVEN)
    turn_group = jnp.where(sp == 0, TURN_FIRST, TURN_LATER)

    def q_cols(g, count=1):
        return pl.ds(pl.multiple_of(g * QW, QW), count * QW)

    def kv_cols(g, count=1):
        return pl.ds(pl.multiple_of(g * KW, KW), count * KW)

    def loads(g, count):
        q, kv = q_cols(g, count), kv_cols(g, count)
        index = 0 if g == 0 else 1
        return [
            pltpu.make_async_copy(kv_hbm.at[0, :, kv], own.at[:, kv], own_sem.at[index]),
            pltpu.make_async_copy(q_hbm.at[0, :, q], q_buf.at[:, q], q_sem.at[index]),
        ]

    def kv_copy(g, source, tile, target, send_sem, count=1):
        cols = kv_cols(g, count)
        return pltpu.make_async_remote_copy(
            src_ref=source.at[:, cols],
            dst_ref=kv_buf.at[tile, :, cols],
            send_sem=send_sem,
            recv_sem=kv_recv.at[tile, g],
            device_id={"sp": target},
            device_id_type=MESH,
        )

    def own_send(g, count=1):
        return kv_copy(g, kv_hbm.at[0], sp, sp + 1, kv_send.at[0], count)

    def direct(g, target):
        return kv_copy(g, kv_hbm.at[0], sp, target, direct_send.at[target - 2])

    def forward(g, tile, count=1):
        return kv_copy(g, kv_buf.at[tile], tile, sp + 1, kv_send.at[tile + 1], count)

    def arrival(g, tile):
        return kv_copy(g, kv_buf.at[tile], tile, sp, kv_send.at[tile + 1])

    def give(source, target, index):
        return pltpu.make_async_remote_copy(
            src_ref=source, dst_ref=target, send_sem=give_send.at[index],
            recv_sem=give_recv.at[index], device_id={"pipe": after}, device_id_type=MESH,
        )

    def gifts():
        return [
            give(q_hbm.at[0, :, q_cols(GIVEN)], q_buf.at[:, q_cols(TAKEN)], 0),
            give(kv_hbm.at[0, :, kv_cols(GIVEN)], own.at[:, kv_cols(TAKEN)], 1),
            give(first_hbm, first_taken, 2),
        ]

    def give_tile(tile):
        return give(
            kv_buf.at[tile, :, kv_cols(GIVEN)], kv_buf.at[tile, :, kv_cols(TAKEN)], 3 + tile
        )

    def out_copy(begin, width):
        cols = pl.ds(pl.multiple_of(begin, DH), width)
        return pltpu.make_async_remote_copy(
            src_ref=staged.at[:, cols],
            dst_ref=out_ref.at[0, :, cols],
            send_sem=out_send,
            recv_sem=out_recv,
            device_id={"pipe": after},
            device_id_type=MESH,
        )

    relay_cols = pl.ds(RELAYED * QW, RW)
    relay_in = pltpu.make_async_remote_copy(
        src_ref=staged.at[:, relay_cols],
        dst_ref=relay_buf,
        send_sem=relay_sems.at[0],
        recv_sem=relay_sems.at[1],
        device_id={"pipe": after, "sp": last},
        device_id_type=MESH,
    )
    relay_out = pltpu.make_async_remote_copy(
        src_ref=relay_buf,
        dst_ref=out_ref.at[0, :, relay_cols],
        send_sem=relay_sems.at[2],
        recv_sem=relay_sems.at[3],
        device_id={"sp": last - 1},
        device_id_type=MESH,
    )

    def send_out(g):
        split = relays & (g == RELAYED)

        @pl.when(jnp.logical_not(split))
        def _():
            out_copy(g * QW, QW).start()

        if relaying:
            @pl.when(split)
            def _():
                out_copy(RELAYED * QW + RW, QW - RW).start()
                relay_in.start()

    taken_copy = pltpu.make_async_copy(
        staged.at[:, q_cols(TAKEN)], out_ref.at[0, :, q_cols(GIVEN)], taken_sem
    )
    barrier = pltpu.get_barrier_semaphore()

    def greet(**where):
        pl.semaphore_signal(barrier, inc=1, device_id=where, device_id_type=MESH)

    for lower in range(last - 1):
        @pl.when((sp > lower if DIRECT else sp == lower + 1) & (sp < last))
        def _():
            greet(sp=lower)
    greet(pipe=before)
    if paired:
        @pl.when(even)
        def _():
            greet(pipe=after)
    if relaying:
        @pl.when(carries)
        def _():
            greet(pipe=before, sp=last - 1)

        @pl.when(relayed)
        def _():
            greet(sp=last)
    greeted = 1 + jnp.where(sends, last - 1 - sp if DIRECT else 1, 0)
    if paired:
        greeted += jnp.where(odd, 1, 0)
    if relaying:
        greeted += jnp.where(relays | carries, 1, 0)
    for load in loads(0, 1):
        load.start()
    first_copy = pltpu.make_async_copy(first_hbm, first_ref, first_sem)
    first_copy.start()

    def send_own(g):
        @pl.when(sends)
        def _():
            if OWN_FIRST:
                own_send(g).start()
            if isinstance(g, int) and g < DIRECT:
                for target in range(last - 1, 1, -1):
                    @pl.when(target > sp + 1)
                    def _():
                        direct(g, target).start()
            if not OWN_FIRST:
                own_send(g).start()

    def enter():
        pl.semaphore_wait(barrier, greeted)
        if paired:
            @pl.when(gives)
            def _():
                for gift in gifts():
                    gift.start()

            @pl.when(sends & even)
            def _():
                pl.semaphore_wait(turn, 1)
        for g in range(DIRECT):
            send_own(g)

        @pl.loop(DIRECT, jnp.where(sp == 0, KVH, ahead))
        def _(g):
            send_own(g)

    def rest_of_loads():
        for load in loads(1, KVH - 1):
            load.start()

    @pl.when(n_before > 0)
    def _():
        enter()
        rest_of_loads()
        first_copy.wait()

    factor = math.log2(math.e) / math.sqrt(DH)
    row_ids = lax.broadcasted_iota(jnp.int32, (rows, rows), 0)
    col_ids = lax.broadcasted_iota(jnp.int32, (rows, rows), 1)

    first_now[0] = 0

    def choose_first(g):
        @pl.when((n_before > 0) & (g < KVH))
        def _():
            first_now[0] = first_ref[0, sp]

        @pl.when(g == TAKEN)
        def _():
            first_now[0] = first_taken[0, sp]

    def bias_of(tile, first):
        return jnp.where(tile >= first, 0.0, -jnp.inf).astype(jnp.float32)

    def whole_softmax(g, count, begin, heads):
        k_cols = pl.ds(pl.multiple_of(g * KW, DH), DH)
        v_cols = pl.ds(pl.multiple_of(g * KW + DH, DH), DH)
        cols = [
            pl.ds(pl.multiple_of(g * QW + (begin + head) * DH, DH), DH)
            for head in range(heads)
        ]
        first = first_now[0] if count else None
        results = attend(
            [q_buf[:, c] for c in cols],
            [kv_buf[tile, :, k_cols] for tile in range(count)] + [own[:, k_cols]],
            [kv_buf[tile, :, v_cols] for tile in range(count)] + [own[:, v_cols]],
            [bias_of(tile, first) for tile in range(count)],
            row_ids <= col_ids, factor,
        )
        for c, result in zip(cols, results):
            staged[:, c] = result

    def running_softmax(g, begin, heads):
        k_cols = pl.ds(pl.multiple_of(g * KW, DH), DH)
        v_cols = pl.ds(pl.multiple_of(g * KW + DH, DH), DH)
        first = first_now[0]

        @pl.loop(begin, begin + heads)
        def _(head):
            cols = pl.ds(pl.multiple_of(g * QW + head * DH, DH), DH)
            query = q_buf[:, cols]
            score = jnp.where(col_ids <= row_ids, scores_of(query, own[:, k_cols]), -jnp.inf)
            largest = jnp.max(score, axis=-1, keepdims=True)
            term = jnp.exp2((score - largest) * factor)
            total = jnp.sum(term, axis=-1, keepdims=True)
            result = jnp.dot(term.astype(jnp.bfloat16), own[:, v_cols],
                             preferred_element_type=jnp.float32)

            def step(tile, carry):
                largest, total, result = carry
                score = scores_of(query, kv_buf[tile, :, k_cols]) + bias_of(tile, first)
                larger = jnp.maximum(largest, jnp.max(score, axis=-1, keepdims=True))
                shrink = jnp.exp2((largest - larger) * factor)
                term = jnp.exp2((score - larger) * factor)
                total = total * shrink + jnp.sum(term, axis=-1, keepdims=True)
                result = result * shrink + jnp.dot(
                    term.astype(jnp.bfloat16), kv_buf[tile, :, v_cols],
                    preferred_element_type=jnp.float32)
                return larger, total, result

            _, total, result = lax.fori_loop(0, n_before, step, (largest, total, result))
            staged[:, cols] = (result / total).astype(jnp.bfloat16)

    def arrive(g):
        for tile in range(last - 1):
            @pl.when(tile < n_before)
            def _():
                arrival(g, tile).wait_recv()

                @pl.when(sends & (g >= DIRECT))
                def _():
                    forward(g, tile).start()

                @pl.when(gives & (g == GIVEN))
                def _():
                    give_tile(tile).start()

        @pl.when((sp > 0) & (g + ahead < KVH))
        def _():
            send_own(g + ahead)
        for wanted, count in ((0, 1), (1, KVH - 1)):
            @pl.when(g == wanted)
            def _():
                for load in loads(wanted, count):
                    load.wait()

    def taken_arrive():
        for gift in gifts():
            gift.wait_recv()
        for tile in range(last - 1):
            @pl.when(tile < n_before)
            def _():
                give_tile(tile).wait_recv()

    def work_out(g, softmax, entering):
        @pl.when(g == 0)
        def _():
            @pl.loop(0, REP // FIRST_HEADS)
            def _(part):
                begin = part * FIRST_HEADS
                softmax(begin, FIRST_HEADS)
                if entering:
                    @pl.when((part == 0) & (n_before == 0))
                    def _():
                        enter()

                out_copy(begin * DH, FIRST_HEADS * DH).start()
                if entering:
                    @pl.when((part == 0) & (n_before == 0))
                    def _():
                        rest_of_loads()

        @pl.when(g > 0)
        def _():
            softmax(0, REP)

            @pl.when(g < KVH)
            def _():
                send_out(g)

            @pl.when(g == TAKEN)
            def _():
                taken_copy.start()

    def group(i):
        shift = jnp.where(takes & (i > TAKEN_AFTER), 2, 1)
        g = jnp.where(takes & (i == TAKEN_AFTER + 1), TAKEN, i - shift)

        @pl.when(g < KVH)
        def _():
            arrive(g)

        if paired:
            @pl.when(g == TAKEN)
            def _():
                taken_arrive()

        choose_first(g)
        computes = jnp.logical_not(gives & (g == GIVEN))
        if last <= UNROLL_TILES:
            for count in range(max(last, 1)):
                @pl.when((n_before == count) & computes)
                def _():
                    work_out(g, functools.partial(whole_softmax, g, count), count == 0)
        else:
            @pl.when(computes)
            def _():
                work_out(g, functools.partial(running_softmax, g), True)
        if paired:
            @pl.when(sends & odd & (g == turn_group))
            def _():
                pl.semaphore_signal(
                    turn, inc=1, device_id={"pipe": before}, device_id_type=MESH
                )

    @pl.loop(1, jnp.where(takes, KVH + 2, KVH + 1))
    def _(i):
        group(i)

    @pl.when(n_before == 0)
    def _():
        first_copy.wait()
    for g in range(DIRECT):
        for target in range(last - 1, 1, -1):
            @pl.when(target > sp + 1)
            def _():
                direct(g, target).wait_send()
    if paired:
        @pl.when(gives)
        def _():
            for gift in gifts():
                gift.wait_send()
            for tile in range(last - 1):
                @pl.when(tile < n_before)
                def _():
                    give_tile(tile).wait_send()

        @pl.when(takes)
        def _():
            taken_copy.wait()

    @pl.when(sends)
    def _():
        own_send(0, KVH).wait_send()
    for tile in range(last - 1):
        @pl.when(sends & (tile < n_before))
        def _():
            forward(DIRECT, tile, KVH - DIRECT).wait_send()

    if relaying:
        @pl.when(carries)
        def _():
            relay_in.wait_recv()
            relay_out.start()
            relay_out.wait_send()

        @pl.when(relays)
        def _():
            relay_in.wait_send()

        @pl.when(relayed)
        def _():
            relay_out.wait_recv()

    for given, cut, width in (
        (gives, relays, KVH * QW - QW - RW),
        (gives, jnp.logical_not(relays), KVH * QW - QW),
        (jnp.logical_not(gives), True, KVH * QW),
    ):
        @pl.when(given & cut)
        def _():
            out_copy(0, width).wait_send()

    for taken, cut, width in (
        (takes, relayed, KVH * QW - QW - RW),
        (takes, jnp.logical_not(relayed), KVH * QW - QW),
        (jnp.logical_not(takes), True, KVH * QW),
    ):
        @pl.when(taken & cut)
        def _():
            out_copy(0, width).wait_recv()


def per_device(n_pipe, n_sp, queries, keys_values, first_tile):
    rows = queries.shape[1]
    tiles = n_sp
    return pl.pallas_call(
        functools.partial(kernel, n_pipe, n_sp),
        out_shape=jax.ShapeDtypeStruct(queries.shape, jnp.bfloat16),
        in_specs=[
            pl.BlockSpec(memory_space=pltpu.HBM),
            pl.BlockSpec(memory_space=pltpu.HBM),
            pl.BlockSpec(memory_space=pltpu.HBM),
        ],
        out_specs=pl.BlockSpec(memory_space=pl.ANY),
        scratch_shapes=[
            pltpu.SMEM(first_tile.shape, jnp.int32),
            pltpu.SMEM(first_tile.shape, jnp.int32),
            pltpu.SMEM((1,), jnp.int32),
            pltpu.VMEM((rows, SLOTS * QW), jnp.bfloat16),
            pltpu.VMEM((rows, SLOTS * KW), jnp.bfloat16),
            pltpu.VMEM((max(tiles - 2, 1), rows, SLOTS * KW), jnp.bfloat16),
            pltpu.VMEM((rows, SLOTS * QW), jnp.bfloat16),
            pltpu.VMEM((rows, RW), jnp.bfloat16),
            pltpu.SemaphoreType.REGULAR,
            pltpu.SemaphoreType.DMA,
            pltpu.SemaphoreType.DMA((2,)),
            pltpu.SemaphoreType.DMA((2,)),
            pltpu.SemaphoreType.DMA((max(tiles - 3, 1),)),
            pltpu.SemaphoreType.DMA((tiles - 1,)),
            pltpu.SemaphoreType.DMA((max(tiles - 2, 1), KVH)),
            pltpu.SemaphoreType.DMA((3 + max(tiles - 2, 1),)),
            pltpu.SemaphoreType.DMA((3 + max(tiles - 2, 1),)),
            pltpu.SemaphoreType.DMA,
            pltpu.SemaphoreType.DMA((4,)),
            pltpu.SemaphoreType.DMA,
            pltpu.SemaphoreType.DMA,
        ],
        compiler_params=pltpu.CompilerParams(
            collective_id=0, has_side_effects=True, vmem_limit_bytes=40 * 1024 * 1024
        ),
    )(
        pltpu.with_memory_space_constraint(first_tile, pltpu.HBM),
        pltpu.with_memory_space_constraint(queries, pltpu.HBM),
        pltpu.with_memory_space_constraint(keys_values, pltpu.HBM),
    )


def solution(mesh):
    sizes = dict(mesh.shape)
    in_specs = (P("pipe", "sp", None), P("pipe", "sp", None), P("pipe", None))
    out_specs = P("pipe", "sp", None)
    return jax.shard_map(
        functools.partial(per_device, sizes["pipe"], sizes["sp"]),
        mesh=mesh, in_specs=in_specs, out_specs=out_specs, check_vma=False,
    )
```

```python
import functools
import math

import jax
import jax.numpy as jnp
from jax import lax
from jax.experimental import pallas as pl
from jax.experimental.pallas import tpu as pltpu
from jax.sharding import PartitionSpec as P

H = 64
KVH = 8
DH = 128
REP = H // KVH
QW = REP * DH
KW = 2 * DH
UNROLL_TILES = 3
DIRECT = 0
OWN_FIRST = True
FIRST_HEADS = 4
AHEAD = 3
AHEAD_EVEN = 2
TURN_FIRST = 1
TURN_LATER = 5
GIVEN = 1
TAKEN = KVH
SLOTS = KVH + 1
TAKEN_AFTER = 2
RELAYED = 3
RELAYED_HEADS = 5
RW = RELAYED_HEADS * DH
MESH = pl.DeviceIdType.MESH


def scores_of(query, key):
    return lax.dot_general(
        query, key, (((1,), (1,)), ((), ())), preferred_element_type=jnp.float32
    )


def attend(queries, keys, values, biases, visible, factor):
    query = jnp.concatenate(queries, axis=0)
    heads = len(queries)
    scores = [scores_of(key, query) for key in keys]
    parts = scores[:-1]
    parts.append(jnp.where(jnp.concatenate([visible] * heads, axis=1), scores[-1], -jnp.inf))
    biases = biases + [0.0]
    largest = functools.reduce(
        jnp.maximum,
        [jnp.max(part, axis=0, keepdims=True) + bias for part, bias in zip(parts, biases)],
    )
    terms = [jnp.exp2((part - (largest - bias)) * factor) for part, bias in zip(parts, biases)]
    total = jnp.sum(functools.reduce(jnp.add, terms), axis=0, keepdims=True)
    result = sum(
        jnp.dot(value.T, term.astype(jnp.bfloat16), preferred_element_type=jnp.float32)
        for value, term in zip(values, terms)
    ) * (1.0 / total)
    rows = queries[0].shape[0]
    return [
        result[:, head * rows:(head + 1) * rows].T.astype(jnp.bfloat16) for head in range(heads)
    ]


def kernel(n_pipe, n_sp, first_hbm, q_hbm, kv_hbm, out_ref, first_ref, first_taken, first_now, q_buf, own,
           kv_buf, staged, relay_buf, turn, ready, first_sem, q_sem, own_sem, direct_send, kv_send, kv_recv,
           give_send, give_recv, taken_sem, relay_sems, out_send, out_recv):
    sp = lax.axis_index("sp")
    pipe = lax.axis_index("pipe")
    after = lax.rem(pipe + 1, n_pipe)
    before = lax.rem(pipe + n_pipe - 1, n_pipe)
    rows = q_hbm.shape[1]
    last = n_sp - 1
    n_before = jnp.where(sp == last, 0, sp)
    sends = sp < last - 1
    paired = n_pipe % 2 == 0
    odd = lax.rem(pipe, 2) == 1
    even = jnp.logical_not(odd)
    gives = odd & (n_before > 0) & paired
    takes = even & (n_before > 0) & paired
    relaying = paired and last > 1
    relays = odd & (sp == last - 1) & relaying
    carries = even & (sp == last) & relaying
    relayed = even & (sp == last - 1) & relaying
    ahead = jnp.where(odd, AHEAD, AHEAD_EVEN)
    turn_group = jnp.where(sp == 0, TURN_FIRST, TURN_LATER)

    def q_cols(g, count=1):
        return pl.ds(pl.multiple_of(g * QW, QW), count * QW)

    def kv_cols(g, count=1):
        return pl.ds(pl.multiple_of(g * KW, KW), count * KW)

    def loads(g, count):
        q, kv = q_cols(g, count), kv_cols(g, count)
        index = 0 if g == 0 else 1
        return [
            pltpu.make_async_copy(kv_hbm.at[0, :, kv], own.at[:, kv], own_sem.at[index]),
            pltpu.make_async_copy(q_hbm.at[0, :, q], q_buf.at[:, q], q_sem.at[index]),
        ]

    def kv_copy(g, source, tile, target, send_sem, count=1):
        cols = kv_cols(g, count)
        return pltpu.make_async_remote_copy(
            src_ref=source.at[:, cols],
            dst_ref=kv_buf.at[tile, :, cols],
            send_sem=send_sem,
            recv_sem=kv_recv.at[tile, g],
            device_id={"sp": target},
            device_id_type=MESH,
        )

    def own_send(g, count=1):
        return kv_copy(g, kv_hbm.at[0], sp, sp + 1, kv_send.at[0], count)

    def direct(g, target):
        return kv_copy(g, kv_hbm.at[0], sp, target, direct_send.at[target - 2])

    def forward(g, tile, count=1):
        return kv_copy(g, kv_buf.at[tile], tile, sp + 1, kv_send.at[tile + 1], count)

    def arrival(g, tile):
        return kv_copy(g, kv_buf.at[tile], tile, sp, kv_send.at[tile + 1])

    def give(source, target, index):
        return pltpu.make_async_remote_copy(
            src_ref=source, dst_ref=target, send_sem=give_send.at[index],
            recv_sem=give_recv.at[index], device_id={"pipe": after}, device_id_type=MESH,
        )

    def gifts():
        return [
            give(q_hbm.at[0, :, q_cols(GIVEN)], q_buf.at[:, q_cols(TAKEN)], 0),
            give(kv_hbm.at[0, :, kv_cols(GIVEN)], own.at[:, kv_cols(TAKEN)], 1),
            give(first_hbm, first_taken, 2),
        ]

    def give_tile(tile):
        return give(
            kv_buf.at[tile, :, kv_cols(GIVEN)], kv_buf.at[tile, :, kv_cols(TAKEN)], 3 + tile
        )

    def out_copy(begin, width):
        cols = pl.ds(pl.multiple_of(begin, DH), width)
        return pltpu.make_async_remote_copy(
            src_ref=staged.at[:, cols],
            dst_ref=out_ref.at[0, :, cols],
            send_sem=out_send,
            recv_sem=out_recv,
            device_id={"pipe": after},
            device_id_type=MESH,
        )

    relay_cols = pl.ds(RELAYED * QW, RW)
    relay_in = pltpu.make_async_remote_copy(
        src_ref=staged.at[:, relay_cols],
        dst_ref=relay_buf,
        send_sem=relay_sems.at[0],
        recv_sem=relay_sems.at[1],
        device_id={"pipe": after, "sp": last},
        device_id_type=MESH,
    )
    relay_out = pltpu.make_async_remote_copy(
        src_ref=relay_buf,
        dst_ref=out_ref.at[0, :, relay_cols],
        send_sem=relay_sems.at[2],
        recv_sem=relay_sems.at[3],
        device_id={"sp": last - 1},
        device_id_type=MESH,
    )

    def send_out(g):
        split = relays & (g == RELAYED)

        @pl.when(jnp.logical_not(split))
        def _():
            out_copy(g * QW, QW).start()

        if relaying:
            @pl.when(split)
            def _():
                out_copy(RELAYED * QW + RW, QW - RW).start()
                pl.semaphore_wait(ready, 1)
                relay_in.start()

    taken_copy = pltpu.make_async_copy(
        staged.at[:, q_cols(TAKEN)], out_ref.at[0, :, q_cols(GIVEN)], taken_sem
    )
    barrier = pltpu.get_barrier_semaphore()

    def greet(**where):
        pl.semaphore_signal(barrier, inc=1, device_id=where, device_id_type=MESH)

    for lower in range(last - 1):
        @pl.when((sp > lower if DIRECT else sp == lower + 1) & (sp < last))
        def _():
            greet(sp=lower)
    greet(pipe=before)
    if paired:
        @pl.when(even)
        def _():
            greet(pipe=after)
    if relaying:
        @pl.when(relays)
        def _():
            greet(pipe=after, sp=last)

        @pl.when(relayed)
        def _():
            greet(sp=last)
    greeted = 1 + jnp.where(sends, last - 1 - sp if DIRECT else 1, 0)
    if paired:
        greeted += jnp.where(odd, 1, 0)
    if relaying:
        greeted += jnp.where(carries, 2, 0)
    for load in loads(0, 1):
        load.start()
    first_copy = pltpu.make_async_copy(first_hbm, first_ref, first_sem)
    first_copy.start()

    def send_own(g):
        @pl.when(sends)
        def _():
            if OWN_FIRST:
                own_send(g).start()
            if isinstance(g, int) and g < DIRECT:
                for target in range(last - 1, 1, -1):
                    @pl.when(target > sp + 1)
                    def _():
                        direct(g, target).start()
            if not OWN_FIRST:
                own_send(g).start()

    def enter():
        pl.semaphore_wait(barrier, greeted)
        if relaying:
            @pl.when(carries)
            def _():
                pl.semaphore_signal(
                    ready, inc=1, device_id={"pipe": before, "sp": last - 1}, device_id_type=MESH
                )
        if paired:
            @pl.when(gives)
            def _():
                for gift in gifts():
                    gift.start()

            @pl.when(sends & even)
            def _():
                pl.semaphore_wait(turn, 1)
        for g in range(DIRECT):
            send_own(g)

        @pl.loop(DIRECT, jnp.where(sp == 0, KVH, ahead))
        def _(g):
            send_own(g)

    def rest_of_loads():
        for load in loads(1, KVH - 1):
            load.start()

    @pl.when(n_before > 0)
    def _():
        enter()
        rest_of_loads()
        first_copy.wait()

    factor = math.log2(math.e) / math.sqrt(DH)
    row_ids = lax.broadcasted_iota(jnp.int32, (rows, rows), 0)
    col_ids = lax.broadcasted_iota(jnp.int32, (rows, rows), 1)

    first_now[0] = 0

    def choose_first(g):
        @pl.when((n_before > 0) & (g < KVH))
        def _():
            first_now[0] = first_ref[0, sp]

        @pl.when(g == TAKEN)
        def _():
            first_now[0] = first_taken[0, sp]

    def bias_of(tile, first):
        return jnp.where(tile >= first, 0.0, -jnp.inf).astype(jnp.float32)

    def whole_softmax(g, count, begin, heads):
        k_cols = pl.ds(pl.multiple_of(g * KW, DH), DH)
        v_cols = pl.ds(pl.multiple_of(g * KW + DH, DH), DH)
        cols = [
            pl.ds(pl.multiple_of(g * QW + (begin + head) * DH, DH), DH)
            for head in range(heads)
        ]
        first = first_now[0] if count else None
        results = attend(
            [q_buf[:, c] for c in cols],
            [kv_buf[tile, :, k_cols] for tile in range(count)] + [own[:, k_cols]],
            [kv_buf[tile, :, v_cols] for tile in range(count)] + [own[:, v_cols]],
            [bias_of(tile, first) for tile in range(count)],
            row_ids <= col_ids, factor,
        )
        for c, result in zip(cols, results):
            staged[:, c] = result

    def running_softmax(g, begin, heads):
        k_cols = pl.ds(pl.multiple_of(g * KW, DH), DH)
        v_cols = pl.ds(pl.multiple_of(g * KW + DH, DH), DH)
        first = first_now[0]

        @pl.loop(begin, begin + heads)
        def _(head):
            cols = pl.ds(pl.multiple_of(g * QW + head * DH, DH), DH)
            query = q_buf[:, cols]
            score = jnp.where(col_ids <= row_ids, scores_of(query, own[:, k_cols]), -jnp.inf)
            largest = jnp.max(score, axis=-1, keepdims=True)
            term = jnp.exp2((score - largest) * factor)
            total = jnp.sum(term, axis=-1, keepdims=True)
            result = jnp.dot(term.astype(jnp.bfloat16), own[:, v_cols],
                             preferred_element_type=jnp.float32)

            def step(tile, carry):
                largest, total, result = carry
                score = scores_of(query, kv_buf[tile, :, k_cols]) + bias_of(tile, first)
                larger = jnp.maximum(largest, jnp.max(score, axis=-1, keepdims=True))
                shrink = jnp.exp2((largest - larger) * factor)
                term = jnp.exp2((score - larger) * factor)
                total = total * shrink + jnp.sum(term, axis=-1, keepdims=True)
                result = result * shrink + jnp.dot(
                    term.astype(jnp.bfloat16), kv_buf[tile, :, v_cols],
                    preferred_element_type=jnp.float32)
                return larger, total, result

            _, total, result = lax.fori_loop(0, n_before, step, (largest, total, result))
            staged[:, cols] = (result / total).astype(jnp.bfloat16)

    def arrive(g):
        for tile in range(last - 1):
            @pl.when(tile < n_before)
            def _():
                arrival(g, tile).wait_recv()

                @pl.when(sends & (g >= DIRECT))
                def _():
                    forward(g, tile).start()

                @pl.when(gives & (g == GIVEN))
                def _():
                    give_tile(tile).start()

        @pl.when((sp > 0) & (g + ahead < KVH))
        def _():
            send_own(g + ahead)
        for wanted, count in ((0, 1), (1, KVH - 1)):
            @pl.when(g == wanted)
            def _():
                for load in loads(wanted, count):
                    load.wait()

    def taken_arrive():
        for gift in gifts():
            gift.wait_recv()
        for tile in range(last - 1):
            @pl.when(tile < n_before)
            def _():
                give_tile(tile).wait_recv()

    def work_out(g, softmax, entering):
        @pl.when(g == 0)
        def _():
            @pl.loop(0, REP // FIRST_HEADS)
            def _(part):
                begin = part * FIRST_HEADS
                softmax(begin, FIRST_HEADS)
                if entering:
                    @pl.when((part == 0) & (n_before == 0))
                    def _():
                        enter()

                out_copy(begin * DH, FIRST_HEADS * DH).start()
                if entering:
                    @pl.when((part == 0) & (n_before == 0))
                    def _():
                        rest_of_loads()

        @pl.when(g > 0)
        def _():
            softmax(0, REP)

            @pl.when(g < KVH)
            def _():
                send_out(g)

            @pl.when(g == TAKEN)
            def _():
                taken_copy.start()

    def group(i):
        shift = jnp.where(takes & (i > TAKEN_AFTER), 2, 1)
        g = jnp.where(takes & (i == TAKEN_AFTER + 1), TAKEN, i - shift)

        @pl.when(g < KVH)
        def _():
            arrive(g)

        if paired:
            @pl.when(g == TAKEN)
            def _():
                taken_arrive()

        choose_first(g)
        computes = jnp.logical_not(gives & (g == GIVEN))
        if last <= UNROLL_TILES:
            for count in range(max(last, 1)):
                @pl.when((n_before == count) & computes)
                def _():
                    work_out(g, functools.partial(whole_softmax, g, count), count == 0)
        else:
            @pl.when(computes)
            def _():
                work_out(g, functools.partial(running_softmax, g), True)
        if paired:
            @pl.when(sends & odd & (g == turn_group))
            def _():
                pl.semaphore_signal(
                    turn, inc=1, device_id={"pipe": before}, device_id_type=MESH
                )

    @pl.loop(1, jnp.where(takes, KVH + 2, KVH + 1))
    def _(i):
        group(i)

    @pl.when(n_before == 0)
    def _():
        first_copy.wait()
    for g in range(DIRECT):
        for target in range(last - 1, 1, -1):
            @pl.when(target > sp + 1)
            def _():
                direct(g, target).wait_send()
    if paired:
        @pl.when(gives)
        def _():
            for gift in gifts():
                gift.wait_send()
            for tile in range(last - 1):
                @pl.when(tile < n_before)
                def _():
                    give_tile(tile).wait_send()

        @pl.when(takes)
        def _():
            taken_copy.wait()

    @pl.when(sends)
    def _():
        own_send(0, KVH).wait_send()
    for tile in range(last - 1):
        @pl.when(sends & (tile < n_before))
        def _():
            forward(DIRECT, tile, KVH - DIRECT).wait_send()

    if relaying:
        @pl.when(carries)
        def _():
            relay_in.wait_recv()
            relay_out.start()
            relay_out.wait_send()

        @pl.when(relays)
        def _():
            relay_in.wait_send()

        @pl.when(relayed)
        def _():
            relay_out.wait_recv()

    for given, cut, width in (
        (gives, relays, KVH * QW - QW - RW),
        (gives, jnp.logical_not(relays), KVH * QW - QW),
        (jnp.logical_not(gives), True, KVH * QW),
    ):
        @pl.when(given & cut)
        def _():
            out_copy(0, width).wait_send()

    for taken, cut, width in (
        (takes, relayed, KVH * QW - QW - RW),
        (takes, jnp.logical_not(relayed), KVH * QW - QW),
        (jnp.logical_not(takes), True, KVH * QW),
    ):
        @pl.when(taken & cut)
        def _():
            out_copy(0, width).wait_recv()


def per_device(n_pipe, n_sp, queries, keys_values, first_tile):
    rows = queries.shape[1]
    tiles = n_sp
    return pl.pallas_call(
        functools.partial(kernel, n_pipe, n_sp),
        out_shape=jax.ShapeDtypeStruct(queries.shape, jnp.bfloat16),
        in_specs=[
            pl.BlockSpec(memory_space=pltpu.HBM),
            pl.BlockSpec(memory_space=pltpu.HBM),
            pl.BlockSpec(memory_space=pltpu.HBM),
        ],
        out_specs=pl.BlockSpec(memory_space=pl.ANY),
        scratch_shapes=[
            pltpu.SMEM(first_tile.shape, jnp.int32),
            pltpu.SMEM(first_tile.shape, jnp.int32),
            pltpu.SMEM((1,), jnp.int32),
            pltpu.VMEM((rows, SLOTS * QW), jnp.bfloat16),
            pltpu.VMEM((rows, SLOTS * KW), jnp.bfloat16),
            pltpu.VMEM((max(tiles - 2, 1), rows, SLOTS * KW), jnp.bfloat16),
            pltpu.VMEM((rows, SLOTS * QW), jnp.bfloat16),
            pltpu.VMEM((rows, RW), jnp.bfloat16),
            pltpu.SemaphoreType.REGULAR,
            pltpu.SemaphoreType.REGULAR,
            pltpu.SemaphoreType.DMA,
            pltpu.SemaphoreType.DMA((2,)),
            pltpu.SemaphoreType.DMA((2,)),
            pltpu.SemaphoreType.DMA((max(tiles - 3, 1),)),
            pltpu.SemaphoreType.DMA((tiles - 1,)),
            pltpu.SemaphoreType.DMA((max(tiles - 2, 1), KVH)),
            pltpu.SemaphoreType.DMA((3 + max(tiles - 2, 1),)),
            pltpu.SemaphoreType.DMA((3 + max(tiles - 2, 1),)),
            pltpu.SemaphoreType.DMA,
            pltpu.SemaphoreType.DMA((4,)),
            pltpu.SemaphoreType.DMA,
            pltpu.SemaphoreType.DMA,
        ],
        compiler_params=pltpu.CompilerParams(
            collective_id=0, has_side_effects=True, vmem_limit_bytes=40 * 1024 * 1024
        ),
    )(
        pltpu.with_memory_space_constraint(first_tile, pltpu.HBM),
        pltpu.with_memory_space_constraint(queries, pltpu.HBM),
        pltpu.with_memory_space_constraint(keys_values, pltpu.HBM),
    )


def solution(mesh):
    sizes = dict(mesh.shape)
    in_specs = (P("pipe", "sp", None), P("pipe", "sp", None), P("pipe", None))
    out_specs = P("pipe", "sp", None)
    return jax.shard_map(
        functools.partial(per_device, sizes["pipe"], sizes["sp"]),
        mesh=mesh, in_specs=in_specs, out_specs=out_specs, check_vma=False,
    )
```

```python
import functools
import math

import jax
import jax.numpy as jnp
from jax import lax
from jax.experimental import pallas as pl
from jax.experimental.pallas import tpu as pltpu
from jax.sharding import PartitionSpec as P

H = 64
KVH = 8
DH = 128
REP = H // KVH
QW = REP * DH
KW = 2 * DH
UNROLL_TILES = 3
DIRECT = 0
OWN_FIRST = True
FIRST_HEADS = 4
ALONE_HEADS = 2
AHEAD = 3
AHEAD_EVEN = 2
TURN_FIRST = 1
TURN_LATER = 5
GIVEN = 1
TAKEN = KVH
SLOTS = KVH + 1
TAKEN_AFTER = 2
RELAYED = 3
RELAYED_HEADS = 5
RW = RELAYED_HEADS * DH
MESH = pl.DeviceIdType.MESH


def scores_of(query, key):
    return lax.dot_general(
        query, key, (((1,), (1,)), ((), ())), preferred_element_type=jnp.float32
    )


def attend(queries, keys, values, biases, visible, factor):
    query = jnp.concatenate(queries, axis=0)
    heads = len(queries)
    scores = [scores_of(key, query) for key in keys]
    parts = scores[:-1]
    parts.append(jnp.where(jnp.concatenate([visible] * heads, axis=1), scores[-1], -jnp.inf))
    biases = biases + [0.0]
    largest = functools.reduce(
        jnp.maximum,
        [jnp.max(part, axis=0, keepdims=True) + bias for part, bias in zip(parts, biases)],
    )
    terms = [jnp.exp2((part - (largest - bias)) * factor) for part, bias in zip(parts, biases)]
    total = jnp.sum(functools.reduce(jnp.add, terms), axis=0, keepdims=True)
    result = sum(
        jnp.dot(value.T, term.astype(jnp.bfloat16), preferred_element_type=jnp.float32)
        for value, term in zip(values, terms)
    ) * (1.0 / total)
    rows = queries[0].shape[0]
    return [
        result[:, head * rows:(head + 1) * rows].T.astype(jnp.bfloat16) for head in range(heads)
    ]


def kernel(n_pipe, n_sp, first_hbm, q_hbm, kv_hbm, out_ref, first_ref, first_taken, first_now, q_buf, own,
           kv_buf, staged, relay_buf, turn, ready, first_sem, q_sem, own_sem, direct_send, kv_send, kv_recv,
           give_send, give_recv, taken_sem, relay_sems, out_send, out_recv):
    sp = lax.axis_index("sp")
    pipe = lax.axis_index("pipe")
    after = lax.rem(pipe + 1, n_pipe)
    before = lax.rem(pipe + n_pipe - 1, n_pipe)
    rows = q_hbm.shape[1]
    last = n_sp - 1
    n_before = jnp.where(sp == last, 0, sp)
    sends = sp < last - 1
    paired = n_pipe % 2 == 0
    odd = lax.rem(pipe, 2) == 1
    even = jnp.logical_not(odd)
    gives = odd & (n_before > 0) & paired
    takes = even & (n_before > 0) & paired
    relaying = paired and last > 1
    relays = odd & (sp == last - 1) & relaying
    carries = even & (sp == last) & relaying
    relayed = even & (sp == last - 1) & relaying
    ahead = jnp.where(odd, AHEAD, AHEAD_EVEN)
    turn_group = jnp.where(sp == 0, TURN_FIRST, TURN_LATER)

    def q_cols(g, count=1):
        return pl.ds(pl.multiple_of(g * QW, QW), count * QW)

    def kv_cols(g, count=1):
        return pl.ds(pl.multiple_of(g * KW, KW), count * KW)

    def loads(g, count):
        q, kv = q_cols(g, count), kv_cols(g, count)
        index = 0 if g == 0 else 1
        return [
            pltpu.make_async_copy(kv_hbm.at[0, :, kv], own.at[:, kv], own_sem.at[index]),
            pltpu.make_async_copy(q_hbm.at[0, :, q], q_buf.at[:, q], q_sem.at[index]),
        ]

    def kv_copy(g, source, tile, target, send_sem, count=1):
        cols = kv_cols(g, count)
        return pltpu.make_async_remote_copy(
            src_ref=source.at[:, cols],
            dst_ref=kv_buf.at[tile, :, cols],
            send_sem=send_sem,
            recv_sem=kv_recv.at[tile, g],
            device_id={"sp": target},
            device_id_type=MESH,
        )

    def own_send(g, count=1):
        return kv_copy(g, kv_hbm.at[0], sp, sp + 1, kv_send.at[0], count)

    def direct(g, target):
        return kv_copy(g, kv_hbm.at[0], sp, target, direct_send.at[target - 2])

    def forward(g, tile, count=1):
        return kv_copy(g, kv_buf.at[tile], tile, sp + 1, kv_send.at[tile + 1], count)

    def arrival(g, tile):
        return kv_copy(g, kv_buf.at[tile], tile, sp, kv_send.at[tile + 1])

    def give(source, target, index):
        return pltpu.make_async_remote_copy(
            src_ref=source, dst_ref=target, send_sem=give_send.at[index],
            recv_sem=give_recv.at[index], device_id={"pipe": after}, device_id_type=MESH,
        )

    def gifts():
        return [
            give(q_hbm.at[0, :, q_cols(GIVEN)], q_buf.at[:, q_cols(TAKEN)], 1),
            give(kv_hbm.at[0, :, kv_cols(GIVEN)], own.at[:, kv_cols(TAKEN)], 1),
            give(first_hbm, first_taken, 0),
        ]

    def give_tile(tile):
        return give(
            kv_buf.at[tile, :, kv_cols(GIVEN)], kv_buf.at[tile, :, kv_cols(TAKEN)], 1
        )

    def all_gifts(method):
        getattr(give(first_hbm, first_taken, 0), method)()
        for count in range(1, last):
            @pl.when(n_before == count)
            def _():
                part = staged.at[:, pl.ds(0, QW + (count + 1) * KW)]
                getattr(give(part, part, 1), method)()

    def out_copy(begin, width):
        cols = pl.ds(pl.multiple_of(begin, DH), width)
        return pltpu.make_async_remote_copy(
            src_ref=staged.at[:, cols],
            dst_ref=out_ref.at[0, :, cols],
            send_sem=out_send,
            recv_sem=out_recv,
            device_id={"pipe": after},
            device_id_type=MESH,
        )

    relay_cols = pl.ds(RELAYED * QW, RW)
    relay_in = pltpu.make_async_remote_copy(
        src_ref=staged.at[:, relay_cols],
        dst_ref=relay_buf,
        send_sem=relay_sems.at[0],
        recv_sem=relay_sems.at[1],
        device_id={"pipe": after, "sp": last},
        device_id_type=MESH,
    )
    relay_out = pltpu.make_async_remote_copy(
        src_ref=relay_buf,
        dst_ref=out_ref.at[0, :, relay_cols],
        send_sem=relay_sems.at[0],
        recv_sem=relay_sems.at[1],
        device_id={"sp": last - 1},
        device_id_type=MESH,
    )

    def send_out(g):
        split = relays & (g == RELAYED)

        @pl.when(jnp.logical_not(split))
        def _():
            out_copy(g * QW, QW).start()

        if relaying:
            @pl.when(split)
            def _():
                out_copy(RELAYED * QW + RW, QW - RW).start()
                pl.semaphore_wait(ready, 1)
                relay_in.start()

    taken_copy = pltpu.make_async_copy(
        staged.at[:, q_cols(TAKEN)], out_ref.at[0, :, q_cols(GIVEN)], taken_sem
    )
    barrier = pltpu.get_barrier_semaphore()

    def greet(**where):
        pl.semaphore_signal(barrier, inc=1, device_id=where, device_id_type=MESH)

    for lower in range(last - 1):
        @pl.when((sp > lower if DIRECT else sp == lower + 1) & (sp < last))
        def _():
            greet(sp=lower)
    greet(pipe=before)
    if paired:
        @pl.when(even)
        def _():
            greet(pipe=after)
    if relaying:
        @pl.when(relays)
        def _():
            greet(pipe=after, sp=last)

        @pl.when(relayed)
        def _():
            greet(sp=last)
    greeted = 1 + jnp.where(sends, last - 1 - sp if DIRECT else 1, 0)
    if paired:
        greeted += jnp.where(odd, 1, 0)
    if relaying:
        greeted += jnp.where(carries, 2, 0)
    for load in loads(0, 1):
        load.start()
    first_copy = pltpu.make_async_copy(first_hbm, first_ref, first_sem)
    first_copy.start()

    def send_own(g):
        @pl.when(sends)
        def _():
            if OWN_FIRST:
                own_send(g).start()
            if isinstance(g, int) and g < DIRECT:
                for target in range(last - 1, 1, -1):
                    @pl.when(target > sp + 1)
                    def _():
                        direct(g, target).start()
            if not OWN_FIRST:
                own_send(g).start()

    def enter():
        pl.semaphore_wait(barrier, greeted)
        if relaying:
            @pl.when(carries)
            def _():
                pl.semaphore_signal(
                    ready, inc=1, device_id={"pipe": before, "sp": last - 1}, device_id_type=MESH
                )
        if paired:
            @pl.when(gives)
            def _():
                for gift in gifts():
                    gift.start()

            @pl.when(sends & even)
            def _():
                pl.semaphore_wait(turn, 1)
        for g in range(DIRECT):
            send_own(g)

        @pl.loop(DIRECT, jnp.where(sp == 0, KVH, ahead))
        def _(g):
            send_own(g)

    def rest_of_loads():
        for load in loads(1, KVH - 1):
            load.start()

    @pl.when(n_before > 0)
    def _():
        enter()
        rest_of_loads()
        first_copy.wait()

    factor = math.log2(math.e) / math.sqrt(DH)
    row_ids = lax.broadcasted_iota(jnp.int32, (rows, rows), 0)
    col_ids = lax.broadcasted_iota(jnp.int32, (rows, rows), 1)

    first_now[0] = 0

    def choose_first(g):
        @pl.when((n_before > 0) & (g < KVH))
        def _():
            first_now[0] = first_ref[0, sp]

        @pl.when(g == TAKEN)
        def _():
            first_now[0] = first_taken[0, sp]

    def bias_of(tile, first):
        return jnp.where(tile >= first, 0.0, -jnp.inf).astype(jnp.float32)

    def whole_softmax(g, count, begin, heads):
        k_cols = pl.ds(pl.multiple_of(g * KW, DH), DH)
        v_cols = pl.ds(pl.multiple_of(g * KW + DH, DH), DH)
        cols = [
            pl.ds(pl.multiple_of(g * QW + (begin + head) * DH, DH), DH)
            for head in range(heads)
        ]
        first = first_now[0] if count else None
        results = attend(
            [q_buf[:, c] for c in cols],
            [kv_buf[tile, :, k_cols] for tile in range(count)] + [own[:, k_cols]],
            [kv_buf[tile, :, v_cols] for tile in range(count)] + [own[:, v_cols]],
            [bias_of(tile, first) for tile in range(count)],
            row_ids <= col_ids, factor,
        )
        for c, result in zip(cols, results):
            staged[:, c] = result

    def running_softmax(g, begin, heads):
        k_cols = pl.ds(pl.multiple_of(g * KW, DH), DH)
        v_cols = pl.ds(pl.multiple_of(g * KW + DH, DH), DH)
        first = first_now[0]

        @pl.loop(begin, begin + heads)
        def _(head):
            cols = pl.ds(pl.multiple_of(g * QW + head * DH, DH), DH)
            query = q_buf[:, cols]
            score = jnp.where(col_ids <= row_ids, scores_of(query, own[:, k_cols]), -jnp.inf)
            largest = jnp.max(score, axis=-1, keepdims=True)
            term = jnp.exp2((score - largest) * factor)
            total = jnp.sum(term, axis=-1, keepdims=True)
            result = jnp.dot(term.astype(jnp.bfloat16), own[:, v_cols],
                             preferred_element_type=jnp.float32)

            def step(tile, carry):
                largest, total, result = carry
                score = scores_of(query, kv_buf[tile, :, k_cols]) + bias_of(tile, first)
                larger = jnp.maximum(largest, jnp.max(score, axis=-1, keepdims=True))
                shrink = jnp.exp2((largest - larger) * factor)
                term = jnp.exp2((score - larger) * factor)
                total = total * shrink + jnp.sum(term, axis=-1, keepdims=True)
                result = result * shrink + jnp.dot(
                    term.astype(jnp.bfloat16), kv_buf[tile, :, v_cols],
                    preferred_element_type=jnp.float32)
                return larger, total, result

            _, total, result = lax.fori_loop(0, n_before, step, (largest, total, result))
            staged[:, cols] = (result / total).astype(jnp.bfloat16)

    def arrive(g):
        for tile in range(last - 1):
            @pl.when(tile < n_before)
            def _():
                arrival(g, tile).wait_recv()

                @pl.when(sends & (g >= DIRECT))
                def _():
                    forward(g, tile).start()

                @pl.when(gives & (g == GIVEN))
                def _():
                    give_tile(tile).start()

        @pl.when((sp > 0) & (g + ahead < KVH))
        def _():
            send_own(g + ahead)
        for wanted, count in ((0, 1), (1, KVH - 1)):
            @pl.when(g == wanted)
            def _():
                for load in loads(wanted, count):
                    load.wait()

    def taken_arrive():
        all_gifts("wait_recv")

    def work_out(g, softmax, entering, first_heads=FIRST_HEADS):
        @pl.when(g == 0)
        def _():
            @pl.loop(0, REP // first_heads)
            def _(part):
                begin = part * first_heads
                softmax(begin, first_heads)
                if entering:
                    @pl.when((part == 0) & (n_before == 0))
                    def _():
                        enter()

                out_copy(begin * DH, first_heads * DH).start()
                if entering:
                    @pl.when((part == 0) & (n_before == 0))
                    def _():
                        rest_of_loads()

        @pl.when(g > 0)
        def _():
            softmax(0, REP)

            @pl.when(g < KVH)
            def _():
                send_out(g)

            @pl.when(g == TAKEN)
            def _():
                taken_copy.start()

    def group(i):
        shift = jnp.where(takes & (i > TAKEN_AFTER), 2, 1)
        g = jnp.where(takes & (i == TAKEN_AFTER + 1), TAKEN, i - shift)

        @pl.when(g < KVH)
        def _():
            arrive(g)

        if paired:
            @pl.when(g == TAKEN)
            def _():
                taken_arrive()

        choose_first(g)
        computes = jnp.logical_not(gives & (g == GIVEN))
        if last <= UNROLL_TILES:
            for count in range(max(last, 1)):
                @pl.when((n_before == count) & computes)
                def _():
                    work_out(
                        g, functools.partial(whole_softmax, g, count), count == 0,
                        FIRST_HEADS if count else ALONE_HEADS,
                    )
        else:
            @pl.when(computes)
            def _():
                work_out(g, functools.partial(running_softmax, g), True)
        if paired:
            @pl.when(sends & odd & (g == turn_group))
            def _():
                pl.semaphore_signal(
                    turn, inc=1, device_id={"pipe": before}, device_id_type=MESH
                )

    @pl.loop(1, jnp.where(takes, KVH + 2, KVH + 1))
    def _(i):
        group(i)

    @pl.when(n_before == 0)
    def _():
        first_copy.wait()
    for g in range(DIRECT):
        for target in range(last - 1, 1, -1):
            @pl.when(target > sp + 1)
            def _():
                direct(g, target).wait_send()
    if paired:
        @pl.when(gives)
        def _():
            all_gifts("wait_send")

        @pl.when(takes)
        def _():
            taken_copy.wait()

    @pl.when(sends)
    def _():
        own_send(0, KVH).wait_send()
    for tile in range(last - 1):
        @pl.when(sends & (tile < n_before))
        def _():
            forward(DIRECT, tile, KVH - DIRECT).wait_send()

    if relaying:
        @pl.when(carries)
        def _():
            relay_in.wait_recv()
            relay_out.start()
            relay_out.wait_send()

        @pl.when(relays)
        def _():
            relay_in.wait_send()

        @pl.when(relayed)
        def _():
            relay_out.wait_recv()

    for given, cut, width in (
        (gives, relays, KVH * QW - QW - RW),
        (gives, jnp.logical_not(relays), KVH * QW - QW),
        (jnp.logical_not(gives), True, KVH * QW),
    ):
        @pl.when(given & cut)
        def _():
            out_copy(0, width).wait_send()

    for taken, cut, width in (
        (takes, relayed, KVH * QW - QW - RW),
        (takes, jnp.logical_not(relayed), KVH * QW - QW),
        (jnp.logical_not(takes), True, KVH * QW),
    ):
        @pl.when(taken & cut)
        def _():
            out_copy(0, width).wait_recv()


def per_device(n_pipe, n_sp, queries, keys_values, first_tile):
    rows = queries.shape[1]
    tiles = n_sp
    return pl.pallas_call(
        functools.partial(kernel, n_pipe, n_sp),
        out_shape=jax.ShapeDtypeStruct(queries.shape, jnp.bfloat16),
        in_specs=[
            pl.BlockSpec(memory_space=pltpu.HBM),
            pl.BlockSpec(memory_space=pltpu.HBM),
            pl.BlockSpec(memory_space=pltpu.HBM),
        ],
        out_specs=pl.BlockSpec(memory_space=pl.ANY),
        scratch_shapes=[
            pltpu.SMEM(first_tile.shape, jnp.int32),
            pltpu.SMEM(first_tile.shape, jnp.int32),
            pltpu.SMEM((1,), jnp.int32),
            pltpu.VMEM((rows, SLOTS * QW), jnp.bfloat16),
            pltpu.VMEM((rows, SLOTS * KW), jnp.bfloat16),
            pltpu.VMEM((max(tiles - 2, 1), rows, SLOTS * KW), jnp.bfloat16),
            pltpu.VMEM((rows, SLOTS * QW), jnp.bfloat16),
            pltpu.VMEM((rows, RW), jnp.bfloat16),
            pltpu.SemaphoreType.REGULAR,
            pltpu.SemaphoreType.REGULAR,
            pltpu.SemaphoreType.DMA,
            pltpu.SemaphoreType.DMA((2,)),
            pltpu.SemaphoreType.DMA((2,)),
            pltpu.SemaphoreType.DMA((max(tiles - 3, 1),)),
            pltpu.SemaphoreType.DMA((tiles - 1,)),
            pltpu.SemaphoreType.DMA((max(tiles - 2, 1), KVH)),
            pltpu.SemaphoreType.DMA((2,)),
            pltpu.SemaphoreType.DMA((2,)),
            pltpu.SemaphoreType.DMA,
            pltpu.SemaphoreType.DMA((2,)),
            pltpu.SemaphoreType.DMA,
            pltpu.SemaphoreType.DMA,
        ],
        compiler_params=pltpu.CompilerParams(
            collective_id=0, has_side_effects=True, vmem_limit_bytes=40 * 1024 * 1024
        ),
    )(
        pltpu.with_memory_space_constraint(first_tile, pltpu.HBM),
        pltpu.with_memory_space_constraint(queries, pltpu.HBM),
        pltpu.with_memory_space_constraint(keys_values, pltpu.HBM),
    )


def solution(mesh):
    sizes = dict(mesh.shape)
    in_specs = (P("pipe", "sp", None), P("pipe", "sp", None), P("pipe", None))
    out_specs = P("pipe", "sp", None)
    return jax.shard_map(
        functools.partial(per_device, sizes["pipe"], sizes["sp"]),
        mesh=mesh, in_specs=in_specs, out_specs=out_specs, check_vma=False,
    )
```

```python
import functools
import math

import jax
import jax.numpy as jnp
from jax import lax
from jax.experimental import pallas as pl
from jax.experimental.pallas import tpu as pltpu
from jax.sharding import PartitionSpec as P

H = 64
KVH = 8
DH = 128
REP = H // KVH
QW = REP * DH
KW = 2 * DH
UNROLL_TILES = 3
DIRECT = 0
FIRST_HEADS = 4
ALONE_HEADS = 2
AHEAD = 3
AHEAD_EVEN = 2
TURN_FIRST = 1
TURN_LATER = 5
GIVEN = 1
TAKEN = KVH
SLOTS = KVH + 1
TAKEN_AFTER = 2
RELAYED = 3
RELAYED_HEADS = 5
RW = RELAYED_HEADS * DH
MESH = pl.DeviceIdType.MESH


def scores_of(query, key):
    return lax.dot_general(
        query, key, (((1,), (1,)), ((), ())), preferred_element_type=jnp.float32
    )


def attend(queries, keys, values, biases, visible, factor):
    query = jnp.concatenate(queries, axis=0)
    heads = len(queries)
    scores = [scores_of(key, query) for key in keys]
    parts = scores[:-1]
    parts.append(jnp.where(jnp.concatenate([visible] * heads, axis=1), scores[-1], -jnp.inf))
    biases = biases + [0.0]
    largest = functools.reduce(
        jnp.maximum,
        [jnp.max(part, axis=0, keepdims=True) + bias for part, bias in zip(parts, biases)],
    )
    terms = [jnp.exp2((part - (largest - bias)) * factor) for part, bias in zip(parts, biases)]
    total = jnp.sum(functools.reduce(jnp.add, terms), axis=0, keepdims=True)
    result = sum(
        jnp.dot(value.T, term.astype(jnp.bfloat16), preferred_element_type=jnp.float32)
        for value, term in zip(values, terms)
    ) * (1.0 / total)
    rows = queries[0].shape[0]
    return [
        result[:, head * rows:(head + 1) * rows].T.astype(jnp.bfloat16) for head in range(heads)
    ]


def kernel(n_pipe, n_sp, first_hbm, q_hbm, kv_hbm, out_ref, first_ref, first_taken, first_now, q_buf, own,
           kv_buf, staged, relay_buf, turn, ready, first_sem, load_sems, kv_send, kv_recv,
           give_send, give_recv, taken_sem, relay_sems, out_send, out_recv):
    sp = lax.axis_index("sp")
    pipe = lax.axis_index("pipe")
    after = lax.rem(pipe + 1, n_pipe)
    before = lax.rem(pipe + n_pipe - 1, n_pipe)
    rows = q_hbm.shape[1]
    last = n_sp - 1
    n_before = jnp.where(sp == last, 0, sp)
    sends = sp < last - 1
    paired = n_pipe % 2 == 0
    odd = lax.rem(pipe, 2) == 1
    even = jnp.logical_not(odd)
    gives = odd & (n_before > 0) & paired
    takes = even & (n_before > 0) & paired
    relaying = paired and last > 1
    relays = odd & (sp == last - 1) & relaying
    carries = even & (sp == last) & relaying
    relayed = even & (sp == last - 1) & relaying
    ahead = jnp.where(odd, AHEAD, AHEAD_EVEN)
    turn_group = jnp.where(sp == 0, TURN_FIRST, TURN_LATER)

    def q_cols(g, count=1):
        return pl.ds(pl.multiple_of(g * QW, QW), count * QW)

    def kv_cols(g, count=1):
        return pl.ds(pl.multiple_of(g * KW, KW), count * KW)

    def loads(g, count):
        q, kv = q_cols(g, count), kv_cols(g, count)
        index = 0 if g == 0 else 1
        return [
            pltpu.make_async_copy(kv_hbm.at[0, :, kv], own.at[:, kv], load_sems.at[index]),
            pltpu.make_async_copy(q_hbm.at[0, :, q], q_buf.at[:, q], load_sems.at[index]),
        ]

    def kv_copy(g, source, tile, target, send_sem, count=1):
        cols = kv_cols(g, count)
        return pltpu.make_async_remote_copy(
            src_ref=source.at[:, cols],
            dst_ref=kv_buf.at[tile, :, cols],
            send_sem=send_sem,
            recv_sem=kv_recv.at[jnp.where(target == last - 1, 0, tile), g],
            device_id={"sp": target},
            device_id_type=MESH,
        )

    def own_send(g, count=1):
        return kv_copy(g, kv_hbm.at[0], sp, sp + 1, kv_send, count)

    def forward(g, tile, count=1):
        return kv_copy(g, kv_buf.at[tile], tile, sp + 1, kv_send, count)

    def arrival(g, tile):
        return kv_copy(g, kv_buf.at[tile], tile, sp, kv_send)

    def give(source, target, index):
        return pltpu.make_async_remote_copy(
            src_ref=source, dst_ref=target, send_sem=give_send.at[index],
            recv_sem=give_recv.at[index], device_id={"pipe": after}, device_id_type=MESH,
        )

    def gifts():
        return [
            give(q_hbm.at[0, :, q_cols(GIVEN)], q_buf.at[:, q_cols(TAKEN)], 1),
            give(kv_hbm.at[0, :, kv_cols(GIVEN)], own.at[:, kv_cols(TAKEN)], 1),
            give(first_hbm, first_taken, 0),
        ]

    def give_tile(tile):
        return give(
            kv_buf.at[tile, :, kv_cols(GIVEN)], kv_buf.at[tile, :, kv_cols(TAKEN)], 1
        )

    def all_gifts(method):
        getattr(give(first_hbm, first_taken, 0), method)()
        for count in range(1, last):
            @pl.when(n_before == count)
            def _():
                part = staged.at[:, pl.ds(0, QW + (count + 1) * KW)]
                getattr(give(part, part, 1), method)()

    def out_copy(begin, width):
        cols = pl.ds(pl.multiple_of(begin, DH), width)
        return pltpu.make_async_remote_copy(
            src_ref=staged.at[:, cols],
            dst_ref=out_ref.at[0, :, cols],
            send_sem=out_send,
            recv_sem=out_recv,
            device_id={"pipe": after},
            device_id_type=MESH,
        )

    relay_cols = pl.ds(RELAYED * QW, RW)
    relay_in = pltpu.make_async_remote_copy(
        src_ref=staged.at[:, relay_cols],
        dst_ref=relay_buf,
        send_sem=relay_sems.at[0],
        recv_sem=relay_sems.at[1],
        device_id={"pipe": after, "sp": last},
        device_id_type=MESH,
    )
    relay_out = pltpu.make_async_remote_copy(
        src_ref=relay_buf,
        dst_ref=out_ref.at[0, :, relay_cols],
        send_sem=relay_sems.at[0],
        recv_sem=relay_sems.at[1],
        device_id={"sp": last - 1},
        device_id_type=MESH,
    )

    def send_out(g):
        split = relays & (g == RELAYED)

        @pl.when(jnp.logical_not(split))
        def _():
            out_copy(g * QW, QW).start()

        if relaying:
            @pl.when(split)
            def _():
                out_copy(RELAYED * QW + RW, QW - RW).start()
                pl.semaphore_wait(ready, 1)
                relay_in.start()

    taken_copy = pltpu.make_async_copy(
        staged.at[:, q_cols(TAKEN)], out_ref.at[0, :, q_cols(GIVEN)], taken_sem
    )
    barrier = pltpu.get_barrier_semaphore()

    def greet(**where):
        pl.semaphore_signal(barrier, inc=1, device_id=where, device_id_type=MESH)

    for lower in range(last - 1):
        @pl.when((sp > lower if DIRECT else sp == lower + 1) & (sp < last))
        def _():
            greet(sp=lower)
    greet(pipe=before)
    if paired:
        @pl.when(even)
        def _():
            greet(pipe=after)
    if relaying:
        @pl.when(relays)
        def _():
            greet(pipe=after, sp=last)

        @pl.when(relayed)
        def _():
            greet(sp=last)
    greeted = 1 + jnp.where(sends, last - 1 - sp if DIRECT else 1, 0)
    if paired:
        greeted += jnp.where(odd, 1, 0)
    if relaying:
        greeted += jnp.where(carries, 2, 0)
    for load in loads(0, 1):
        load.start()
    first_copy = pltpu.make_async_copy(first_hbm, first_ref, first_sem)
    first_copy.start()

    def send_own(g):
        @pl.when(sends)
        def _():
            own_send(g).start()

    def enter():
        pl.semaphore_wait(barrier, greeted)
        if relaying:
            @pl.when(carries)
            def _():
                pl.semaphore_signal(
                    ready, inc=1, device_id={"pipe": before, "sp": last - 1}, device_id_type=MESH
                )
        if paired:
            @pl.when(gives)
            def _():
                for gift in gifts():
                    gift.start()

            @pl.when(sends & even)
            def _():
                pl.semaphore_wait(turn, 1)
        for g in range(DIRECT):
            send_own(g)

        @pl.loop(DIRECT, jnp.where(sp == 0, KVH, ahead))
        def _(g):
            send_own(g)

    def rest_of_loads():
        for load in loads(1, KVH - 1):
            load.start()

    @pl.when(n_before > 0)
    def _():
        enter()
        rest_of_loads()
        first_copy.wait()

    factor = math.log2(math.e) / math.sqrt(DH)
    row_ids = lax.broadcasted_iota(jnp.int32, (rows, rows), 0)
    col_ids = lax.broadcasted_iota(jnp.int32, (rows, rows), 1)

    first_now[0] = 0

    def choose_first(g):
        @pl.when((n_before > 0) & (g < KVH))
        def _():
            first_now[0] = first_ref[0, sp]

        @pl.when(g == TAKEN)
        def _():
            first_now[0] = first_taken[0, sp]

    def bias_of(tile, first):
        return jnp.where(tile >= first, 0.0, -jnp.inf).astype(jnp.float32)

    def whole_softmax(g, count, begin, heads):
        k_cols = pl.ds(pl.multiple_of(g * KW, DH), DH)
        v_cols = pl.ds(pl.multiple_of(g * KW + DH, DH), DH)
        cols = [
            pl.ds(pl.multiple_of(g * QW + (begin + head) * DH, DH), DH)
            for head in range(heads)
        ]
        first = first_now[0] if count else None
        results = attend(
            [q_buf[:, c] for c in cols],
            [kv_buf[tile, :, k_cols] for tile in range(count)] + [own[:, k_cols]],
            [kv_buf[tile, :, v_cols] for tile in range(count)] + [own[:, v_cols]],
            [bias_of(tile, first) for tile in range(count)],
            row_ids <= col_ids, factor,
        )
        for c, result in zip(cols, results):
            staged[:, c] = result

    def running_softmax(g, begin, heads):
        k_cols = pl.ds(pl.multiple_of(g * KW, DH), DH)
        v_cols = pl.ds(pl.multiple_of(g * KW + DH, DH), DH)
        first = first_now[0]

        @pl.loop(begin, begin + heads)
        def _(head):
            cols = pl.ds(pl.multiple_of(g * QW + head * DH, DH), DH)
            query = q_buf[:, cols]
            score = jnp.where(col_ids <= row_ids, scores_of(query, own[:, k_cols]), -jnp.inf)
            largest = jnp.max(score, axis=-1, keepdims=True)
            term = jnp.exp2((score - largest) * factor)
            total = jnp.sum(term, axis=-1, keepdims=True)
            result = jnp.dot(term.astype(jnp.bfloat16), own[:, v_cols],
                             preferred_element_type=jnp.float32)

            def step(tile, carry):
                largest, total, result = carry
                score = scores_of(query, kv_buf[tile, :, k_cols]) + bias_of(tile, first)
                larger = jnp.maximum(largest, jnp.max(score, axis=-1, keepdims=True))
                shrink = jnp.exp2((largest - larger) * factor)
                term = jnp.exp2((score - larger) * factor)
                total = total * shrink + jnp.sum(term, axis=-1, keepdims=True)
                result = result * shrink + jnp.dot(
                    term.astype(jnp.bfloat16), kv_buf[tile, :, v_cols],
                    preferred_element_type=jnp.float32)
                return larger, total, result

            _, total, result = lax.fori_loop(0, n_before, step, (largest, total, result))
            staged[:, cols] = (result / total).astype(jnp.bfloat16)

    def whole_wait(tiles, cols, recv_sem):
        part = kv_buf.at[pl.ds(0, tiles), :, pl.ds(0, cols)]
        return pltpu.make_async_remote_copy(
            src_ref=part, dst_ref=part, send_sem=kv_send, recv_sem=recv_sem,
            device_id={"pipe": after}, device_id_type=MESH,
        )

    def arrive(g):
        if last > 1:
            @pl.when(sp == last - 1)
            def _():
                whole_wait(last - 1, KW, kv_recv.at[0, g]).wait_recv()
                for tile in range(last - 1):
                    @pl.when(gives & (g == GIVEN))
                    def _():
                        give_tile(tile).start()

        for tile in range(last - 2):
            @pl.when((tile < n_before) & (sp < last - 1))
            def _():
                arrival(g, tile).wait_recv()

                @pl.when(sends & (g >= DIRECT))
                def _():
                    forward(g, tile).start()

                @pl.when(gives & (g == GIVEN))
                def _():
                    give_tile(tile).start()

        @pl.when((sp > 0) & (g + ahead < KVH))
        def _():
            send_own(g + ahead)
        for wanted, count in ((0, 1), (1, KVH - 1)):
            @pl.when(g == wanted)
            def _():
                part = pl.ds(0, count * (QW + KW))
                pltpu.make_async_copy(
                    staged.at[:, part], q_buf.at[:, part], load_sems.at[min(wanted, 1)]
                ).wait()

    def taken_arrive():
        all_gifts("wait_recv")

    def work_out(g, softmax, entering, first_heads=FIRST_HEADS):
        @pl.when(g == 0)
        def _():
            @pl.loop(0, REP // first_heads)
            def _(part):
                begin = part * first_heads
                softmax(begin, first_heads)
                if entering:
                    @pl.when((part == 0) & (n_before == 0))
                    def _():
                        enter()

                out_copy(begin * DH, first_heads * DH).start()
                if entering:
                    @pl.when((part == 0) & (n_before == 0))
                    def _():
                        rest_of_loads()

        @pl.when(g > 0)
        def _():
            softmax(0, REP)

            @pl.when(g < KVH)
            def _():
                send_out(g)

            @pl.when(g == TAKEN)
            def _():
                taken_copy.start()

    def group(i):
        shift = jnp.where(takes & (i > TAKEN_AFTER), 2, 1)
        g = jnp.where(takes & (i == TAKEN_AFTER + 1), TAKEN, i - shift)

        @pl.when(g < KVH)
        def _():
            arrive(g)

        if paired:
            @pl.when(g == TAKEN)
            def _():
                taken_arrive()

        choose_first(g)
        computes = jnp.logical_not(gives & (g == GIVEN))
        if last <= UNROLL_TILES:
            for count in range(max(last, 1)):
                @pl.when((n_before == count) & computes)
                def _():
                    work_out(
                        g, functools.partial(whole_softmax, g, count), count == 0,
                        FIRST_HEADS if count else ALONE_HEADS,
                    )
        else:
            @pl.when(computes)
            def _():
                work_out(g, functools.partial(running_softmax, g), True)
        if paired:
            @pl.when(sends & odd & (g == turn_group))
            def _():
                pl.semaphore_signal(
                    turn, inc=1, device_id={"pipe": before}, device_id_type=MESH
                )

    @pl.loop(1, jnp.where(takes, KVH + 2, KVH + 1))
    def _(i):
        group(i)

    @pl.when(n_before == 0)
    def _():
        first_copy.wait()
    if paired:
        @pl.when(gives)
        def _():
            all_gifts("wait_send")

        @pl.when(takes)
        def _():
            taken_copy.wait()

    for lower in range(last - 1):
        @pl.when(sp == lower)
        def _():
            whole_wait(lower + 1, KVH * KW, kv_recv.at[0, 0]).wait_send()

    if relaying:
        @pl.when(carries)
        def _():
            relay_in.wait_recv()
            relay_out.start()
            relay_out.wait_send()

        @pl.when(relays)
        def _():
            relay_in.wait_send()

        @pl.when(relayed)
        def _():
            relay_out.wait_recv()

    for given, cut, width in (
        (gives, relays, KVH * QW - QW - RW),
        (gives, jnp.logical_not(relays), KVH * QW - QW),
        (jnp.logical_not(gives), True, KVH * QW),
    ):
        @pl.when(given & cut)
        def _():
            out_copy(0, width).wait_send()

    for taken, cut, width in (
        (takes, relayed, KVH * QW - QW - RW),
        (takes, jnp.logical_not(relayed), KVH * QW - QW),
        (jnp.logical_not(takes), True, KVH * QW),
    ):
        @pl.when(taken & cut)
        def _():
            out_copy(0, width).wait_recv()


def per_device(n_pipe, n_sp, queries, keys_values, first_tile):
    rows = queries.shape[1]
    tiles = n_sp
    return pl.pallas_call(
        functools.partial(kernel, n_pipe, n_sp),
        out_shape=jax.ShapeDtypeStruct(queries.shape, jnp.bfloat16),
        in_specs=[
            pl.BlockSpec(memory_space=pltpu.HBM),
            pl.BlockSpec(memory_space=pltpu.HBM),
            pl.BlockSpec(memory_space=pltpu.HBM),
        ],
        out_specs=pl.BlockSpec(memory_space=pl.ANY),
        scratch_shapes=[
            pltpu.SMEM(first_tile.shape, jnp.int32),
            pltpu.SMEM(first_tile.shape, jnp.int32),
            pltpu.SMEM((1,), jnp.int32),
            pltpu.VMEM((rows, SLOTS * QW), jnp.bfloat16),
            pltpu.VMEM((rows, SLOTS * KW), jnp.bfloat16),
            pltpu.VMEM((max(tiles - 2, 1), rows, SLOTS * KW), jnp.bfloat16),
            pltpu.VMEM((rows, SLOTS * QW), jnp.bfloat16),
            pltpu.VMEM((rows, RW), jnp.bfloat16),
            pltpu.SemaphoreType.REGULAR,
            pltpu.SemaphoreType.REGULAR,
            pltpu.SemaphoreType.DMA,
            pltpu.SemaphoreType.DMA((2,)),
            pltpu.SemaphoreType.DMA,
            pltpu.SemaphoreType.DMA((max(tiles - 3, 1), KVH)),
            pltpu.SemaphoreType.DMA((2,)),
            pltpu.SemaphoreType.DMA((2,)),
            pltpu.SemaphoreType.DMA,
            pltpu.SemaphoreType.DMA((2,)),
            pltpu.SemaphoreType.DMA,
            pltpu.SemaphoreType.DMA,
        ],
        compiler_params=pltpu.CompilerParams(
            collective_id=0, has_side_effects=True, vmem_limit_bytes=40 * 1024 * 1024
        ),
    )(
        pltpu.with_memory_space_constraint(first_tile, pltpu.HBM),
        pltpu.with_memory_space_constraint(queries, pltpu.HBM),
        pltpu.with_memory_space_constraint(keys_values, pltpu.HBM),
    )


def solution(mesh):
    sizes = dict(mesh.shape)
    in_specs = (P("pipe", "sp", None), P("pipe", "sp", None), P("pipe", None))
    out_specs = P("pipe", "sp", None)
    return jax.shard_map(
        functools.partial(per_device, sizes["pipe"], sizes["sp"]),
        mesh=mesh, in_specs=in_specs, out_specs=out_specs, check_vma=False,
    )
```

```python
import functools
import math

import jax
import jax.numpy as jnp
from jax import lax
from jax.experimental import pallas as pl
from jax.experimental.pallas import tpu as pltpu
from jax.sharding import PartitionSpec as P

H = 64
KVH = 8
DH = 128
REP = H // KVH
QW = REP * DH
KW = 2 * DH
UNROLL_TILES = 3
DIRECT = 0
FIRST_HEADS = 4
ALONE_HEADS = 2
AHEAD = 3
AHEAD_EVEN = 2
TURN_FIRST = 1
TURN_LATER = 5
GIVEN = 1
TAKEN = KVH
SLOTS = KVH + 1
TAKEN_AFTER = 2
RELAYED = 3
RELAYED_HEADS = 5
RW = RELAYED_HEADS * DH
LOWERED = 4
MESH = pl.DeviceIdType.MESH


def scores_of(query, key):
    return lax.dot_general(
        query, key, (((1,), (1,)), ((), ())), preferred_element_type=jnp.float32
    )


def attend(queries, keys, values, biases, visible, factor):
    query = jnp.concatenate(queries, axis=0)
    heads = len(queries)
    scores = [scores_of(key, query) for key in keys]
    parts = scores[:-1]
    parts.append(jnp.where(jnp.concatenate([visible] * heads, axis=1), scores[-1], -jnp.inf))
    biases = biases + [0.0]
    largest = functools.reduce(
        jnp.maximum,
        [jnp.max(part, axis=0, keepdims=True) + bias for part, bias in zip(parts, biases)],
    )
    terms = [jnp.exp2((part - (largest - bias)) * factor) for part, bias in zip(parts, biases)]
    total = jnp.sum(functools.reduce(jnp.add, terms), axis=0, keepdims=True)
    result = sum(
        jnp.dot(value.T, term.astype(jnp.bfloat16), preferred_element_type=jnp.float32)
        for value, term in zip(values, terms)
    ) * (1.0 / total)
    rows = queries[0].shape[0]
    return [
        result[:, head * rows:(head + 1) * rows].T.astype(jnp.bfloat16) for head in range(heads)
    ]


def kernel(n_pipe, n_sp, first_hbm, q_hbm, kv_hbm, out_ref, first_ref, first_taken, first_now, q_buf, own,
           kv_buf, staged, relay_buf, low_buf, turn, ready, first_sem, load_sems, kv_send, kv_recv,
           give_send, give_recv, taken_sem, relay_sems, low_sems, out_send, out_recv):
    sp = lax.axis_index("sp")
    pipe = lax.axis_index("pipe")
    after = lax.rem(pipe + 1, n_pipe)
    before = lax.rem(pipe + n_pipe - 1, n_pipe)
    rows = q_hbm.shape[1]
    last = n_sp - 1
    n_before = jnp.where(sp == last, 0, sp)
    sends = sp < last - 1
    paired = n_pipe % 2 == 0
    odd = lax.rem(pipe, 2) == 1
    even = jnp.logical_not(odd)
    gives = odd & (n_before > 0) & paired
    takes = even & (n_before > 0) & paired
    relaying = paired and last > 2
    relays = odd & (sp == last - 1) & relaying
    carries = even & (sp == last) & relaying
    relayed = even & (sp == last - 1) & relaying
    ahead = jnp.where(odd, AHEAD, AHEAD_EVEN)
    turn_group = jnp.where(sp == 0, TURN_FIRST, TURN_LATER)

    def q_cols(g, count=1):
        return pl.ds(pl.multiple_of(g * QW, QW), count * QW)

    def kv_cols(g, count=1):
        return pl.ds(pl.multiple_of(g * KW, KW), count * KW)

    def loads(g, count):
        q, kv = q_cols(g, count), kv_cols(g, count)
        index = 0 if g == 0 else 1
        return [
            pltpu.make_async_copy(kv_hbm.at[0, :, kv], own.at[:, kv], load_sems.at[index]),
            pltpu.make_async_copy(q_hbm.at[0, :, q], q_buf.at[:, q], load_sems.at[index]),
        ]

    def kv_copy(g, source, tile, target, send_sem, count=1):
        cols = kv_cols(g, count)
        return pltpu.make_async_remote_copy(
            src_ref=source.at[:, cols],
            dst_ref=kv_buf.at[tile, :, cols],
            send_sem=send_sem,
            recv_sem=kv_recv.at[jnp.where(target == last - 1, 0, tile), g],
            device_id={"sp": target},
            device_id_type=MESH,
        )

    def own_send(g, count=1):
        return kv_copy(g, kv_hbm.at[0], sp, sp + 1, kv_send, count)

    def forward(g, tile, count=1):
        return kv_copy(g, kv_buf.at[tile], tile, sp + 1, kv_send, count)

    def arrival(g, tile):
        return kv_copy(g, kv_buf.at[tile], tile, sp, kv_send)

    def give(source, target, index):
        return pltpu.make_async_remote_copy(
            src_ref=source, dst_ref=target, send_sem=give_send.at[index],
            recv_sem=give_recv.at[index], device_id={"pipe": after}, device_id_type=MESH,
        )

    def gifts():
        return [
            give(q_hbm.at[0, :, q_cols(GIVEN)], q_buf.at[:, q_cols(TAKEN)], 1),
            give(kv_hbm.at[0, :, kv_cols(GIVEN)], own.at[:, kv_cols(TAKEN)], 1),
            give(first_hbm, first_taken, 0),
        ]

    def give_tile(tile):
        return give(
            kv_buf.at[tile, :, kv_cols(GIVEN)], kv_buf.at[tile, :, kv_cols(TAKEN)], 1
        )

    def all_gifts(method):
        getattr(give(first_hbm, first_taken, 0), method)()
        for count in range(1, last):
            @pl.when(n_before == count)
            def _():
                part = staged.at[:, pl.ds(0, QW + (count + 1) * KW)]
                getattr(give(part, part, 1), method)()

    def out_copy(begin, width):
        cols = pl.ds(pl.multiple_of(begin, DH), width)
        return pltpu.make_async_remote_copy(
            src_ref=staged.at[:, cols],
            dst_ref=out_ref.at[0, :, cols],
            send_sem=out_send,
            recv_sem=out_recv,
            device_id={"pipe": after},
            device_id_type=MESH,
        )

    relay_cols = pl.ds(RELAYED * QW, RW)
    relay_in = pltpu.make_async_remote_copy(
        src_ref=staged.at[:, relay_cols],
        dst_ref=relay_buf,
        send_sem=relay_sems.at[0],
        recv_sem=relay_sems.at[1],
        device_id={"pipe": after, "sp": last},
        device_id_type=MESH,
    )
    relay_out = pltpu.make_async_remote_copy(
        src_ref=relay_buf,
        dst_ref=out_ref.at[0, :, relay_cols],
        send_sem=relay_sems.at[0],
        recv_sem=relay_sems.at[1],
        device_id={"sp": last - 1},
        device_id_type=MESH,
    )

    low_cols = pl.ds(LOWERED * QW, DH)
    low_in = pltpu.make_async_remote_copy(
        src_ref=staged.at[:, low_cols], dst_ref=low_buf, send_sem=low_sems.at[0],
        recv_sem=low_sems.at[1], device_id={"pipe": after, "sp": last - 2}, device_id_type=MESH,
    )
    low_out = pltpu.make_async_remote_copy(
        src_ref=low_buf, dst_ref=out_ref.at[0, :, low_cols], send_sem=low_sems.at[0],
        recv_sem=low_sems.at[1], device_id={"sp": last - 1}, device_id_type=MESH,
    )
    lowers = even & (sp == last - 2) & relaying

    def send_out(g):
        lowered = relays & (g == LOWERED)
        split = relays & (g == RELAYED)

        @pl.when(jnp.logical_not(split | lowered))
        def _():
            out_copy(g * QW, QW).start()

        if relaying:
            @pl.when(lowered)
            def _():
                low_in.start()
                out_copy(LOWERED * QW + DH, QW - DH).start()

            @pl.when(split)
            def _():
                out_copy(RELAYED * QW + RW, QW - RW).start()
                pl.semaphore_wait(ready, 1)
                relay_in.start()

    taken_copy = pltpu.make_async_copy(
        staged.at[:, q_cols(TAKEN)], out_ref.at[0, :, q_cols(GIVEN)], taken_sem
    )
    barrier = pltpu.get_barrier_semaphore()

    def greet(**where):
        pl.semaphore_signal(barrier, inc=1, device_id=where, device_id_type=MESH)

    for lower in range(last - 1):
        @pl.when((sp > lower if DIRECT else sp == lower + 1) & (sp < last))
        def _():
            greet(sp=lower)
    greet(pipe=before)
    if paired:
        @pl.when(even)
        def _():
            greet(pipe=after)
    if relaying:
        @pl.when(relays)
        def _():
            greet(pipe=after, sp=last)

        @pl.when(relayed)
        def _():
            greet(sp=last)

        @pl.when(lowers)
        def _():
            greet(pipe=before, sp=last - 1)
    greeted = 1 + jnp.where(sends, last - 1 - sp if DIRECT else 1, 0)
    if paired:
        greeted += jnp.where(odd, 1, 0)
    if relaying:
        greeted += jnp.where(carries, 2, 0) + jnp.where(relays, 1, 0)
    for load in loads(0, 1):
        load.start()
    first_copy = pltpu.make_async_copy(first_hbm, first_ref, first_sem)
    first_copy.start()

    def send_own(g):
        @pl.when(sends)
        def _():
            own_send(g).start()

    def enter():
        pl.semaphore_wait(barrier, greeted)
        if relaying:
            @pl.when(carries)
            def _():
                pl.semaphore_signal(
                    ready, inc=1, device_id={"pipe": before, "sp": last - 1}, device_id_type=MESH
                )
        if paired:
            @pl.when(gives)
            def _():
                for gift in gifts():
                    gift.start()

            @pl.when(sends & even)
            def _():
                pl.semaphore_wait(turn, 1)
        for g in range(DIRECT):
            send_own(g)

        @pl.loop(DIRECT, jnp.where(sp == 0, KVH, ahead))
        def _(g):
            send_own(g)

    def rest_of_loads():
        for load in loads(1, KVH - 1):
            load.start()

    @pl.when(n_before > 0)
    def _():
        enter()
        rest_of_loads()
        first_copy.wait()

    factor = math.log2(math.e) / math.sqrt(DH)
    row_ids = lax.broadcasted_iota(jnp.int32, (rows, rows), 0)
    col_ids = lax.broadcasted_iota(jnp.int32, (rows, rows), 1)

    first_now[0] = 0

    def choose_first(g):
        @pl.when((n_before > 0) & (g < KVH))
        def _():
            first_now[0] = first_ref[0, sp]

        @pl.when(g == TAKEN)
        def _():
            first_now[0] = first_taken[0, sp]

    def bias_of(tile, first):
        return jnp.where(tile >= first, 0.0, -jnp.inf).astype(jnp.float32)

    def whole_softmax(g, count, begin, heads):
        k_cols = pl.ds(pl.multiple_of(g * KW, DH), DH)
        v_cols = pl.ds(pl.multiple_of(g * KW + DH, DH), DH)
        cols = [
            pl.ds(pl.multiple_of(g * QW + (begin + head) * DH, DH), DH)
            for head in range(heads)
        ]
        first = first_now[0] if count else None
        results = attend(
            [q_buf[:, c] for c in cols],
            [kv_buf[tile, :, k_cols] for tile in range(count)] + [own[:, k_cols]],
            [kv_buf[tile, :, v_cols] for tile in range(count)] + [own[:, v_cols]],
            [bias_of(tile, first) for tile in range(count)],
            row_ids <= col_ids, factor,
        )
        for c, result in zip(cols, results):
            staged[:, c] = result

    def running_softmax(g, begin, heads):
        k_cols = pl.ds(pl.multiple_of(g * KW, DH), DH)
        v_cols = pl.ds(pl.multiple_of(g * KW + DH, DH), DH)
        first = first_now[0]

        @pl.loop(begin, begin + heads)
        def _(head):
            cols = pl.ds(pl.multiple_of(g * QW + head * DH, DH), DH)
            query = q_buf[:, cols]
            score = jnp.where(col_ids <= row_ids, scores_of(query, own[:, k_cols]), -jnp.inf)
            largest = jnp.max(score, axis=-1, keepdims=True)
            term = jnp.exp2((score - largest) * factor)
            total = jnp.sum(term, axis=-1, keepdims=True)
            result = jnp.dot(term.astype(jnp.bfloat16), own[:, v_cols],
                             preferred_element_type=jnp.float32)

            def step(tile, carry):
                largest, total, result = carry
                score = scores_of(query, kv_buf[tile, :, k_cols]) + bias_of(tile, first)
                larger = jnp.maximum(largest, jnp.max(score, axis=-1, keepdims=True))
                shrink = jnp.exp2((largest - larger) * factor)
                term = jnp.exp2((score - larger) * factor)
                total = total * shrink + jnp.sum(term, axis=-1, keepdims=True)
                result = result * shrink + jnp.dot(
                    term.astype(jnp.bfloat16), kv_buf[tile, :, v_cols],
                    preferred_element_type=jnp.float32)
                return larger, total, result

            _, total, result = lax.fori_loop(0, n_before, step, (largest, total, result))
            staged[:, cols] = (result / total).astype(jnp.bfloat16)

    def whole_wait(tiles, cols, recv_sem):
        part = kv_buf.at[pl.ds(0, tiles), :, pl.ds(0, cols)]
        return pltpu.make_async_remote_copy(
            src_ref=part, dst_ref=part, send_sem=kv_send, recv_sem=recv_sem,
            device_id={"pipe": after}, device_id_type=MESH,
        )

    def arrive(g):
        if last > 1:
            @pl.when(sp == last - 1)
            def _():
                whole_wait(last - 1, KW, kv_recv.at[0, g]).wait_recv()
                for tile in range(last - 1):
                    @pl.when(gives & (g == GIVEN))
                    def _():
                        give_tile(tile).start()

        for tile in range(last - 2):
            @pl.when((tile < n_before) & (sp < last - 1))
            def _():
                arrival(g, tile).wait_recv()

                @pl.when(sends & (g >= DIRECT))
                def _():
                    forward(g, tile).start()

                @pl.when(gives & (g == GIVEN))
                def _():
                    give_tile(tile).start()

        @pl.when((sp > 0) & (g + ahead < KVH))
        def _():
            send_own(g + ahead)
        for wanted, count in ((0, 1), (1, KVH - 1)):
            @pl.when(g == wanted)
            def _():
                part = pl.ds(0, count * (QW + KW))
                pltpu.make_async_copy(
                    staged.at[:, part], q_buf.at[:, part], load_sems.at[min(wanted, 1)]
                ).wait()

    def taken_arrive():
        all_gifts("wait_recv")

    def work_out(g, softmax, entering, first_heads=FIRST_HEADS):
        @pl.when(g == 0)
        def _():
            @pl.loop(0, REP // first_heads)
            def _(part):
                begin = part * first_heads
                softmax(begin, first_heads)
                if entering:
                    @pl.when((part == 0) & (n_before == 0))
                    def _():
                        enter()

                out_copy(begin * DH, first_heads * DH).start()
                if entering:
                    @pl.when((part == 0) & (n_before == 0))
                    def _():
                        rest_of_loads()

        @pl.when(g > 0)
        def _():
            softmax(0, REP)

            @pl.when(g < KVH)
            def _():
                send_out(g)

            @pl.when(g == TAKEN)
            def _():
                taken_copy.start()

    def group(i):
        shift = jnp.where(takes & (i > TAKEN_AFTER), 2, 1)
        g = jnp.where(takes & (i == TAKEN_AFTER + 1), TAKEN, i - shift)

        @pl.when(g < KVH)
        def _():
            arrive(g)

        if paired:
            @pl.when(g == TAKEN)
            def _():
                taken_arrive()

        choose_first(g)
        computes = jnp.logical_not(gives & (g == GIVEN))
        if last <= UNROLL_TILES:
            for count in range(max(last, 1)):
                @pl.when((n_before == count) & computes)
                def _():
                    work_out(
                        g, functools.partial(whole_softmax, g, count), count == 0,
                        FIRST_HEADS if count else ALONE_HEADS,
                    )
        else:
            @pl.when(computes)
            def _():
                work_out(g, functools.partial(running_softmax, g), True)
        if paired:
            @pl.when(sends & odd & (g == turn_group))
            def _():
                pl.semaphore_signal(
                    turn, inc=1, device_id={"pipe": before}, device_id_type=MESH
                )

    @pl.loop(1, jnp.where(takes, KVH + 2, KVH + 1))
    def _(i):
        group(i)

    @pl.when(n_before == 0)
    def _():
        first_copy.wait()
    if paired:
        @pl.when(gives)
        def _():
            all_gifts("wait_send")

        @pl.when(takes)
        def _():
            taken_copy.wait()

    for lower in range(last - 1):
        @pl.when(sp == lower)
        def _():
            whole_wait(lower + 1, KVH * KW, kv_recv.at[0, 0]).wait_send()

    if relaying:
        @pl.when(carries)
        def _():
            relay_in.wait_recv()
            relay_out.start()
            relay_out.wait_send()

        @pl.when(relays)
        def _():
            relay_in.wait_send()
            low_in.wait_send()

        @pl.when(lowers)
        def _():
            low_in.wait_recv()
            low_out.start()
            low_out.wait_send()

        @pl.when(relayed)
        def _():
            relay_out.wait_recv()
            low_out.wait_recv()

    for given, cut, width in (
        (gives, relays, KVH * QW - QW - RW - DH),
        (gives, jnp.logical_not(relays), KVH * QW - QW),
        (jnp.logical_not(gives), True, KVH * QW),
    ):
        @pl.when(given & cut)
        def _():
            out_copy(0, width).wait_send()

    for taken, cut, width in (
        (takes, relayed, KVH * QW - QW - RW - DH),
        (takes, jnp.logical_not(relayed), KVH * QW - QW),
        (jnp.logical_not(takes), True, KVH * QW),
    ):
        @pl.when(taken & cut)
        def _():
            out_copy(0, width).wait_recv()


def per_device(n_pipe, n_sp, queries, keys_values, first_tile):
    rows = queries.shape[1]
    tiles = n_sp
    return pl.pallas_call(
        functools.partial(kernel, n_pipe, n_sp),
        out_shape=jax.ShapeDtypeStruct(queries.shape, jnp.bfloat16),
        in_specs=[
            pl.BlockSpec(memory_space=pltpu.HBM),
            pl.BlockSpec(memory_space=pltpu.HBM),
            pl.BlockSpec(memory_space=pltpu.HBM),
        ],
        out_specs=pl.BlockSpec(memory_space=pl.ANY),
        scratch_shapes=[
            pltpu.SMEM(first_tile.shape, jnp.int32),
            pltpu.SMEM(first_tile.shape, jnp.int32),
            pltpu.SMEM((1,), jnp.int32),
            pltpu.VMEM((rows, SLOTS * QW), jnp.bfloat16),
            pltpu.VMEM((rows, SLOTS * KW), jnp.bfloat16),
            pltpu.VMEM((max(tiles - 2, 1), rows, SLOTS * KW), jnp.bfloat16),
            pltpu.VMEM((rows, SLOTS * QW), jnp.bfloat16),
            pltpu.VMEM((rows, RW), jnp.bfloat16),
            pltpu.VMEM((rows, DH), jnp.bfloat16),
            pltpu.SemaphoreType.REGULAR,
            pltpu.SemaphoreType.REGULAR,
            pltpu.SemaphoreType.DMA,
            pltpu.SemaphoreType.DMA((2,)),
            pltpu.SemaphoreType.DMA,
            pltpu.SemaphoreType.DMA((max(tiles - 3, 1), KVH)),
            pltpu.SemaphoreType.DMA((2,)),
            pltpu.SemaphoreType.DMA((2,)),
            pltpu.SemaphoreType.DMA,
            pltpu.SemaphoreType.DMA((2,)),
            pltpu.SemaphoreType.DMA((2,)),
            pltpu.SemaphoreType.DMA,
            pltpu.SemaphoreType.DMA,
        ],
        compiler_params=pltpu.CompilerParams(
            collective_id=0, has_side_effects=True, vmem_limit_bytes=40 * 1024 * 1024
        ),
    )(
        pltpu.with_memory_space_constraint(first_tile, pltpu.HBM),
        pltpu.with_memory_space_constraint(queries, pltpu.HBM),
        pltpu.with_memory_space_constraint(keys_values, pltpu.HBM),
    )


def solution(mesh):
    sizes = dict(mesh.shape)
    in_specs = (P("pipe", "sp", None), P("pipe", "sp", None), P("pipe", None))
    out_specs = P("pipe", "sp", None)
    return jax.shard_map(
        functools.partial(per_device, sizes["pipe"], sizes["sp"]),
        mesh=mesh, in_specs=in_specs, out_specs=out_specs, check_vma=False,
    )
```
